32 devices in a mesh: uly: 8 (over z, y), blk: 4 (over x, core).
Axes of the slice: x: 2, y: 2, z: 4, core: 2. Of those that a mesh axis runs over, the one named last changes fastest.
Arguments:
- queries: bfloat16 [4096, 4096], P(('blk', 'uly')), may hold values from -8 to 8
- keys: bfloat16 [4096, 1024], P(('blk', 'uly')), may hold values from -8 to 8
- values: bfloat16 [4096, 1024], P(('blk', 'uly')), may hold values from -6 to 6
- live_blocks: int32 [32, 8], replicated, may hold values from 0 to 31, as said below
Outputs:
- attended: bfloat16 [4096, 4096], P(('blk', 'uly'))
The draws below stay inside these ranges and needn't reach their ends.
Inputs may be any that keep to these rules, and one draw needn't show every extreme that they name: `live_blocks`: each row holds 8 different block numbers, among them the row's own block, the blocks just before and after it where they exist, and block 0; the others are drawn from the seed.
All inputs are finite; a program needn't handle non-finite values.
Results may differ from the reference program's by a relative error of at most 0.0049.
Values may be sent and summed in bfloat16 or wider, within the bound.
A program may use at most 128 MiB of HBM per device.

```python
import math
import jax
import jax.numpy as jnp
from jax import lax

H = 32
KVH = 8
HD = 128
BLOCK = 128
LIVE = 8
TOKENS = 4096
NB = 32


def drawn_part(key, shape):
    return jax.random.truncated_normal(key, -6.0, 6.0, shape, jnp.float32)


def draw_queries(key, part):
    shape = (TOKENS, H * HD)
    result = drawn_part(jax.random.fold_in(key, 21), shape)
    return result.astype(jnp.bfloat16)


def draw_keys(key, part):
    shape = (TOKENS, KVH * HD)
    result = drawn_part(jax.random.fold_in(key, 22), shape)
    return result.astype(jnp.bfloat16)


def draw_live_blocks(key, part):
    row_ids = jnp.arange(NB, dtype=jnp.int32)[:, None]
    col_ids = jnp.arange(NB, dtype=jnp.int32)[None, :]
    noise = jax.random.randint(jax.random.fold_in(key, 31), (NB, NB), 0, 65536, dtype=jnp.int32)
    forced = (jnp.abs(col_ids - row_ids) <= 1) | (col_ids == 0)
    priority = noise * NB + col_ids + jnp.where(forced, 1 << 28, 0)
    return lax.top_k(priority, LIVE)[1].astype(jnp.int32)


def block_levels(own_key, extent, cuts, least, largest):
    def one(axis_at, shards_of):
        draws = jax.random.uniform(jax.random.fold_in(jax.random.fold_in(own_key, 6), axis_at), (shards_of,), jnp.float32, least / len(cuts), largest / len(cuts))
        return jnp.repeat(jnp.exp(draws), extent[axis_at] // shards_of).reshape((-1,) + (1,) * (len(extent) - axis_at - 1))

    factor_of = one(*cuts[0])
    for cut in cuts[1:]:
        factor_of = factor_of * one(*cut)
    return factor_of


def bell_draw(rng, extent, scale, reach, cuts=(), kind=jnp.bfloat16):
    entries = jax.random.normal(rng, extent, jnp.float32) * scale
    if len(cuts) > 0:
        entries = block_levels(rng, extent, cuts, -0.22, 0.18) * entries
    return jnp.clip(entries, min=-reach, max=reach).astype(kind)


def setup_inputs(seed: int = 0) -> dict:
    arg_keys = jax.random.split(jax.random.key(seed), 5)
    queries = draw_queries(jax.random.fold_in(arg_keys[4], 71), 0)
    keys = draw_keys(jax.random.fold_in(arg_keys[4], 71), 0)
    values = bell_draw(arg_keys[2], (TOKENS, KVH * HD), 1.0, 6.0, ((0, 32),))
    live_blocks = draw_live_blocks(jax.random.fold_in(arg_keys[4], 71), 0)
    return dict(queries=queries, keys=keys, values=values, live_blocks=live_blocks)


def reference(queries, keys, values, live_blocks):
    share = H // KVH
    score_scale = 1.0 / math.sqrt(HD)
    query_blocks = queries.reshape(NB, BLOCK, KVH, share, HD)
    key_blocks = keys.reshape(NB, BLOCK, KVH, HD)
    value_blocks = values.reshape(NB, BLOCK, KVH, HD)

    def attend_block(block_index):
        live_rows = live_blocks[block_index]
        query_block = query_blocks[block_index].astype(jnp.float32)
        key_rows = key_blocks[live_rows].astype(jnp.float32)
        value_rows = value_blocks[live_rows].astype(jnp.float32)
        scores = jnp.einsum('qgrd,lkgd->qgrlk', query_block, key_rows) * score_scale
        row_max = lax.optimization_barrier(jnp.max(scores, axis=(3, 4), keepdims=True))
        weights = jnp.exp(scores - row_max)
        denominator = lax.optimization_barrier(jnp.sum(weights, axis=(3, 4)))
        rounded = lax.optimization_barrier(weights.astype(jnp.bfloat16))
        numerator = jnp.einsum('qgrlk,lkgd->qgrd', rounded.astype(jnp.float32), value_rows)
        return (numerator / denominator[..., None]).astype(jnp.bfloat16)
    attended = lax.map(attend_block, jnp.arange(NB, dtype=jnp.int32))
    return attended.reshape(TOKENS, H * HD)
```

```python
import math

import jax
import jax.numpy as jnp
from jax import lax
from jax.experimental import pallas as pl
from jax.experimental.pallas import tpu as pltpu
from jax.sharding import PartitionSpec as P

HD = 128
CORES = 2
SIDE = 2
CHIPS = SIDE * SIDE
GROUP = CHIPS * CORES
MESH = pl.DeviceIdType.MESH


class Layout:
    def __init__(self, n_uly, n_blk):
        self.n_uly = n_uly
        self.nx = n_blk // CORES
        self.ny = 2 ** (int(math.log2(n_uly)) // 2)
        self.nz = n_uly // self.ny
        self.columns = n_uly * n_blk // GROUP

    def split(self, uly, blk):
        x, core = blk // CORES, blk % CORES
        z, y = uly // self.ny, uly % self.ny
        column = ((x // SIDE) * (self.ny // SIDE) + y // SIDE) * self.nz + z
        return column, (x % SIDE) * SIDE + y % SIDE, core

    def join(self, column, chip, core):
        z, square = column % self.nz, column // self.nz
        x = (square // (self.ny // SIDE)) * SIDE + chip // SIDE
        y = (square % (self.ny // SIDE)) * SIDE + chip % SIDE
        return z * self.ny + y, x * CORES + core

    def slot(self, block):
        column, chip, core = self.split(block % self.n_uly, block // self.n_uly)
        return column * GROUP + core * CHIPS + chip


def partner(chip, rel):
    a = (chip // 2 + rel // 2) % 2
    b = (chip % 2 + rel % 2) % 2
    return a * 2 + b


def kernel(lay, live_hbm, q_ref, k_ref, v_ref, o_ref,
           live_ref, live_sem, qbuf, ka, va, kb, vb, pbuf, lbuf, obuf,
           plane_send, plane_recv, own_sem, z_send, z_recv, c_send, c_recv, o_send, o_recv):
    heads = k_ref.shape[1] // HD // CHIPS
    width = q_ref.shape[1] // CHIPS // heads
    share = width // HD
    live = live_ref.shape[0]
    last = lay.columns - 1
    bufs = ((ka, va), (kb, vb))
    pieces = [(head, kind) for head in range(heads) for kind in range(2)]
    column, chip, core = lay.split(lax.axis_index("uly"), lax.axis_index("blk"))

    def device(col, which, core_of):
        uly, blk = lay.join(col, which, core_of)
        return {"uly": uly, "blk": blk}

    has_down, has_up = column > 0, column < last
    down, up = jnp.maximum(column - 1, 0), jnp.minimum(column + 1, last)
    targets = (device(down, chip, core), device(up, chip, core), device(column, chip, 1 - core))

    barrier = pltpu.get_barrier_semaphore()
    for rel in range(1, CHIPS):
        pl.semaphore_signal(
            barrier, inc=1, device_id=device(column, partner(chip, rel), core), device_id_type=MESH
        )
    pl.semaphore_signal(barrier, inc=1, device_id=targets[2], device_id_type=MESH)

    @pl.when(has_down)
    def _():
        pl.semaphore_signal(barrier, inc=1, device_id=targets[0], device_id_type=MESH)

    @pl.when(has_up)
    def _():
        pl.semaphore_signal(barrier, inc=1, device_id=targets[1], device_id_type=MESH)

    def cols(index, size):
        return pl.ds(pl.multiple_of(index * size, size), size)

    def slot_of(col, item, core_of):
        return col * GROUP + core_of * CHIPS + item

    here = slot_of(column, chip, core)

    def route(head, kind, rel):
        src, dst, size = (
            (k_ref, bufs[head][0].at[here], HD),
            (v_ref, bufs[head][1].at[here], HD),
            (q_ref, qbuf.at[head, rel], width),
        )[kind]
        return src.at[:, cols(partner(chip, rel) * heads + head, size)], dst

    def own(head, kind):
        src, dst = route(head, kind, 0)
        return pltpu.make_async_copy(src, dst, own_sem.at[head, kind])

    def plane(head, kind, rel):
        src, dst = route(head, kind, rel)
        return pltpu.make_async_remote_copy(
            src, dst, plane_send.at[head, kind, rel], plane_recv.at[head, kind, rel],
            device_id=device(column, partner(chip, rel), core), device_id_type=MESH,
        )

    order = [(0, 0), (0, 1)]
    for head in range(1, heads):
        order += [(head, 0), (head - 1, 2), (head, 1)]
    order.append((heads - 1, 2))

    fetch = pltpu.make_async_copy(live_hbm, live_ref, live_sem)
    for head, kind in order:
        own(head, kind).start()
    fetch.start()
    pl.semaphore_wait(barrier, CHIPS + has_down.astype(jnp.int32) + has_up.astype(jnp.int32))

    def chunk(p, col, core_of):
        head, kind = pieces[p]
        return bufs[head][kind].at[pl.ds(slot_of(col, 0, core_of), CHIPS)]

    def hop(p, way, col):
        ref = chunk(p, col, core)
        return pltpu.make_async_remote_copy(
            ref, ref, z_send.at[p, way, col], z_recv.at[p, col],
            device_id=targets[way], device_id_type=MESH,
        )

    def cross(p, col, core_of):
        ref = chunk(p, col, core_of)
        return pltpu.make_async_remote_copy(
            ref, ref, c_send.at[p, col], c_recv.at[p, col],
            device_id=targets[2], device_id_type=MESH,
        )

    def leave(p, way, rel):
        head, kind = pieces[p]
        ref = bufs[head][kind].at[slot_of(column, partner(chip, rel), core)]
        src = route(head, kind, 0)[0] if rel == 0 else ref
        return pltpu.make_async_remote_copy(
            src, ref, z_send.at[p, way, column], z_recv.at[p, column],
            device_id=targets[way], device_id_type=MESH,
        )

    def leave_both(p, rel):
        @pl.when(has_down)
        def _():
            leave(p, 0, rel).start()

        @pl.when(has_up)
        def _():
            leave(p, 1, rel).start()

    def first(p):
        head, kind = pieces[p]
        if p > 0:
            leave_both(p, 0)
        for rel in range(1, CHIPS):
            plane(head, kind, rel).wait_recv()
            leave_both(p, rel)
        own(head, kind).wait()
        cross(p, column, core).start()

    def relay(p, step):
        above, below = column + step, column - step

        @pl.when((step > 0) & (below >= 0))
        def _():
            hop(p, 1, below).wait_recv()

            @pl.when(has_up)
            def _():
                hop(p, 1, below).start()

            cross(p, below, core).start()

        @pl.when((step > 0) & (above <= last))
        def _():
            hop(p, 0, above).wait_recv()

            @pl.when(has_down)
            def _():
                hop(p, 0, above).start()

            cross(p, above, core).start()

    def crossed(p):
        @pl.loop(0, lay.columns)
        def _(col):
            cross(p, col, 1 - core).wait_recv()

    factor = math.log2(math.e) / math.sqrt(HD)

    def picked(buf, rel):
        uly, blk = lay.join(column, partner(chip, rel), core)
        block = blk * lay.n_uly + uly
        return jnp.concatenate([buf[lay.slot(live_ref[i, block])] for i in range(live)], axis=0)

    def weigh(head, rel):
        queries = jnp.concatenate(
            [qbuf[head, rel, :, r * HD:(r + 1) * HD] for r in range(share)], axis=0
        )
        scores = lax.dot_general(
            queries, picked(bufs[head][0], rel), (((1,), (1,)), ((), ())),
            preferred_element_type=jnp.float32,
        )
        row_max = jnp.max(scores, axis=1, keepdims=True)
        weights = jnp.exp2((scores - row_max) * factor)
        total = jnp.sum(weights, axis=1, keepdims=True)
        lbuf[rel] = jnp.broadcast_to(total, lbuf.shape[1:])
        pbuf[rel] = weights.astype(jnp.bfloat16)

    def out_cols(head):
        return cols(chip * heads + head, width)

    def back(head, rel):
        return pltpu.make_async_remote_copy(
            obuf.at[head, rel], o_ref.at[:, out_cols(head)], o_send.at[head, rel], o_recv.at[head, rel],
            device_id=device(column, partner(chip, rel), core), device_id_type=MESH,
        )

    def attend(head, rel):
        product = jnp.dot(pbuf[rel], picked(bufs[head][1], rel), preferred_element_type=jnp.float32)
        result = (product / lbuf[rel]).astype(jnp.bfloat16)
        rows = result.shape[0] // share
        obuf[head, rel] = jnp.concatenate([result[r * rows:(r + 1) * rows] for r in range(share)], axis=1)

        @pl.when(rel > 0)
        def _():
            back(head, rel).start()

        @pl.when(rel == 0)
        def _():
            pltpu.make_async_copy(obuf.at[head, 0], o_ref.at[:, out_cols(head)], o_send.at[head, 0]).start()

    def ready(p):
        head, kind = pieces[p]
        crossed(p)
        if kind == 0:
            own(head, 2).wait()
            for rel in range(1, CHIPS):
                plane(head, 2, rel).wait_recv()

    def unit(p, step):
        head, kind = pieces[p]
        if kind == 0:
            weigh(head, step)
        else:
            attend(head, CHIPS - 1 - step)

    leave_both(0, 0)
    for head, kind in order:
        for rel in range(1, CHIPS):
            plane(head, kind, rel).start()
    first(0)
    fetch.wait()
    for p in range(len(pieces)):
        if p + 1 < len(pieces):
            first(p + 1)
        if p > 0:
            ready(p - 1)

        @pl.loop(0, CHIPS)
        def _(step):
            if p > 0:
                unit(p - 1, step)
            relay(p, step)

        if lay.columns > CHIPS:
            @pl.loop(CHIPS, lay.columns)
            def _(step):
                relay(p, step)

    ready(len(pieces) - 1)

    @pl.loop(0, CHIPS)
    def _(step):
        unit(len(pieces) - 1, step)

    for head in range(heads):
        for kind in range(3):
            for rel in range(1, CHIPS):
                plane(head, kind, rel).wait_send()

    @pl.loop(0, lay.columns)
    def _(col):
        for p in range(len(pieces)):
            @pl.when((col >= column) & has_down)
            def _():
                hop(p, 0, col).wait_send()

            @pl.when((col <= column) & has_up)
            def _():
                hop(p, 1, col).wait_send()

            cross(p, col, core).wait_send()

    for head in range(heads):
        pltpu.make_async_copy(obuf.at[head, 0], o_ref.at[:, out_cols(head)], o_send.at[head, 0]).wait()
        for rel in range(1, CHIPS):
            back(head, rel).wait()


def hand_out(src, dst, sem):
    parts = sem.shape[0]
    rows = src.shape[0] // parts
    copies = [
        pltpu.make_async_copy(src.at[pl.ds(i * rows, rows)], dst.at[pl.ds(i * rows, rows)], sem.at[i])
        for i in range(parts)
    ]
    for copy in copies:
        copy.start()
    for copy in copies:
        copy.wait()


def solution(mesh):
    lay = Layout(mesh.shape["uly"], mesh.shape["blk"])

    def body(queries, keys, values, live_blocks):
        rows, hidden = queries.shape
        heads = keys.shape[1] // HD // CHIPS
        width = hidden // CHIPS // heads
        share = width // HD
        slots = lay.columns * GROUP
        keys_seen = live_blocks.shape[1] * rows
        bf16, f32 = jnp.bfloat16, jnp.float32
        dma = pltpu.SemaphoreType.DMA

        def call(*refs):
            kernel(lay, *refs)

        held = pl.pallas_call(
            call,
            out_shape=pltpu.VMEM((rows, hidden), bf16),
            in_specs=[pl.BlockSpec(memory_space=pltpu.HBM)] * 4,
            out_specs=pl.BlockSpec(memory_space=pltpu.VMEM),
            scratch_shapes=[
                pltpu.SMEM(live_blocks.shape[::-1], live_blocks.dtype),
                dma,
                pltpu.VMEM((heads, CHIPS, rows, width), bf16),
                *[pltpu.VMEM((slots, rows, HD), bf16) for _ in range(4)],
                pltpu.VMEM((CHIPS, rows * share, keys_seen), bf16),
                pltpu.VMEM((CHIPS, rows * share, HD), f32),
                pltpu.VMEM((heads, CHIPS, rows, width), bf16),
                dma((heads, 3, CHIPS)),
                dma((heads, 3, CHIPS)),
                dma((heads, 3)),
                dma((heads * 2, 2, lay.columns)),
                dma((heads * 2, lay.columns)),
                dma((heads * 2, lay.columns)),
                dma((heads * 2, lay.columns)),
                dma((heads, CHIPS)),
                dma((heads, CHIPS)),
            ],
            compiler_params=pltpu.CompilerParams(
                collective_id=0, has_side_effects=True, vmem_limit_bytes=59 * 2**20
            ),
            name="group_attention",
        )(live_blocks.T, queries, keys, values)
        return pl.pallas_call(
            hand_out,
            out_shape=jax.ShapeDtypeStruct((rows, hidden), bf16),
            in_specs=[pl.BlockSpec(memory_space=pl.ANY)],
            out_specs=pl.BlockSpec(memory_space=pl.ANY),
            scratch_shapes=[dma((8,))],
            compiler_params=pltpu.CompilerParams(vmem_limit_bytes=2**20),
            name="hand_out",
        )(held)

    spec = P(("blk", "uly"), None)
    return jax.shard_map(
        body, mesh=mesh, in_specs=(spec, spec, spec, P()), out_specs=spec, check_vma=False
    )
```

```python
import math

import jax
import jax.numpy as jnp
from jax import lax
from jax.experimental import pallas as pl
from jax.experimental.pallas import tpu as pltpu
from jax.sharding import PartitionSpec as P

HD = 128
CORES = 2
SIDE = 2
CHIPS = SIDE * SIDE
GROUP = CHIPS * CORES
MESH = pl.DeviceIdType.MESH


class Layout:
    def __init__(self, n_uly, n_blk):
        self.n_uly = n_uly
        self.nx = n_blk // CORES
        self.ny = 2 ** (int(math.log2(n_uly)) // 2)
        self.nz = n_uly // self.ny
        self.columns = n_uly * n_blk // GROUP

    def split(self, uly, blk):
        x, core = blk // CORES, blk % CORES
        z, y = uly // self.ny, uly % self.ny
        column = ((x // SIDE) * (self.ny // SIDE) + y // SIDE) * self.nz + z
        return column, (x % SIDE) * SIDE + y % SIDE, core

    def join(self, column, chip, core):
        z, square = column % self.nz, column // self.nz
        x = (square // (self.ny // SIDE)) * SIDE + chip // SIDE
        y = (square % (self.ny // SIDE)) * SIDE + chip % SIDE
        return z * self.ny + y, x * CORES + core

    def slot(self, block):
        column, chip, core = self.split(block % self.n_uly, block // self.n_uly)
        return column * GROUP + core * CHIPS + chip


def partner(chip, rel):
    a = (chip // 2 + rel // 2) % 2
    b = (chip % 2 + rel % 2) % 2
    return a * 2 + b


def cut(heads):
    pieces = []
    for head in range(heads - 1):
        pieces += [(head, 0, 0, HD), (head, 1, 0, HD)]
    pieces.append((heads - 1, 0, 0, HD))
    low = 0
    for size in (HD // 2, HD // 4, HD // 4):
        pieces.append((heads - 1, 1, low, size))
        low += size
    return pieces


def turns(piece, heads):
    return piece[0] == heads - 1 and piece[1] == 1


def kernel(lay, live_hbm, q_ref, k_ref, v_ref, o_ref,
           live_ref, live_sem, qbuf, bufs, vin, vturn, pbuf, lbuf, obuf,
           plane_send, plane_recv, own_sem, in_sem, z_send, z_recv, c_send, c_recv, o_send, o_recv):
    heads = k_ref.shape[1] // HD // CHIPS
    width = q_ref.shape[1] // CHIPS // heads
    share = width // HD
    live = live_ref.shape[0]
    last = lay.columns - 1
    pieces = cut(heads)
    count = len(pieces)
    turned = [p for p in range(count) if turns(pieces[p], heads)]
    column, chip, core = lay.split(lax.axis_index("uly"), lax.axis_index("blk"))

    def device(col, which, core_of):
        uly, blk = lay.join(col, which, core_of)
        return {"uly": uly, "blk": blk}

    has_down, has_up = column > 0, column < last
    down, up = jnp.maximum(column - 1, 0), jnp.minimum(column + 1, last)
    targets = (device(down, chip, core), device(up, chip, core), device(column, chip, 1 - core))

    barrier = pltpu.get_barrier_semaphore()
    for rel in range(1, CHIPS):
        pl.semaphore_signal(
            barrier, inc=1, device_id=device(column, partner(chip, rel), core), device_id_type=MESH
        )
    pl.semaphore_signal(barrier, inc=1, device_id=targets[2], device_id_type=MESH)

    @pl.when(has_down)
    def _():
        pl.semaphore_signal(barrier, inc=1, device_id=targets[0], device_id_type=MESH)

    @pl.when(has_up)
    def _():
        pl.semaphore_signal(barrier, inc=1, device_id=targets[1], device_id_type=MESH)

    def cols(index, size):
        return pl.ds(pl.multiple_of(index * size, size), size)

    def slot_of(col, item, core_of):
        return col * GROUP + core_of * CHIPS + item

    here = slot_of(column, chip, core)

    def route(item, rel):
        if item >= count:
            head = item - count
            src = q_ref.at[:, cols(partner(chip, rel) * heads + head, width)]
            return src, qbuf.at[head, rel]
        head, kind, low, size = pieces[item]
        if item in turned:
            return vturn.at[rel, pl.ds(low, size)], bufs[item].at[here]
        src = (k_ref, v_ref)[kind].at[:, cols(partner(chip, rel) * heads + head, HD)]
        return src, bufs[item].at[here]

    def own(item):
        src, dst = route(item, 0)
        return pltpu.make_async_copy(src, dst, own_sem.at[item])

    def plane(item, rel):
        src, dst = route(item, rel)
        return pltpu.make_async_remote_copy(
            src, dst, plane_send.at[item, rel], plane_recv.at[item, rel],
            device_id=device(column, partner(chip, rel), core), device_id_type=MESH,
        )

    def take(rel):
        src = v_ref.at[:, cols(partner(chip, rel) * heads + heads - 1, HD)]
        return pltpu.make_async_copy(src, vin.at[rel], in_sem.at[rel])

    straight = [p for p in range(count) if p not in turned]
    early = straight + [count + head for head in range(heads - 1)]
    late = turned + [count + heads - 1]

    fetch = pltpu.make_async_copy(live_hbm, live_ref, live_sem)
    for rel in range(CHIPS):
        take(rel).start()
    for item in early + late:
        own(item).start() if item not in turned else None
    fetch.start()
    pl.semaphore_wait(barrier, CHIPS + has_down.astype(jnp.int32) + has_up.astype(jnp.int32))

    def chunk(p, col, core_of):
        return bufs[p].at[pl.ds(slot_of(col, 0, core_of), CHIPS)]

    def hop(p, way, col):
        ref = chunk(p, col, core)
        return pltpu.make_async_remote_copy(
            ref, ref, z_send.at[p, way, col], z_recv.at[p, col],
            device_id=targets[way], device_id_type=MESH,
        )

    def cross(p, col, core_of):
        ref = chunk(p, col, core_of)
        return pltpu.make_async_remote_copy(
            ref, ref, c_send.at[p, col], c_recv.at[p, col],
            device_id=targets[2], device_id_type=MESH,
        )

    def leave(p, way, rel):
        ref = bufs[p].at[slot_of(column, partner(chip, rel), core)]
        src = route(p, 0)[0] if rel == 0 else ref
        return pltpu.make_async_remote_copy(
            src, ref, z_send.at[p, way, column], z_recv.at[p, column],
            device_id=targets[way], device_id_type=MESH,
        )

    def leave_both(p, rel):
        @pl.when(has_down)
        def _():
            leave(p, 0, rel).start()

        @pl.when(has_up)
        def _():
            leave(p, 1, rel).start()

    def first(p):
        for rel in range(1, CHIPS):
            plane(p, rel).wait_recv()
            leave_both(p, rel)
        own(p).wait()
        cross(p, column, core).start()

    def relay(p, step):
        above, below = column + step, column - step

        @pl.when((step > 0) & (below >= 0))
        def _():
            hop(p, 1, below).wait_recv()

            @pl.when(has_up)
            def _():
                hop(p, 1, below).start()

            cross(p, below, core).start()

        @pl.when((step > 0) & (above <= last))
        def _():
            hop(p, 0, above).wait_recv()

            @pl.when(has_down)
            def _():
                hop(p, 0, above).start()

            cross(p, above, core).start()

    def crossed(p):
        @pl.loop(0, lay.columns)
        def _(col):
            cross(p, col, 1 - core).wait_recv()

    factor = math.log2(math.e) / math.sqrt(HD)

    def picked(p, rel):
        uly, blk = lay.join(column, partner(chip, rel), core)
        row = blk * lay.n_uly + uly
        axis = 1 if p in turned else 0
        return jnp.concatenate([bufs[p][lay.slot(live_ref[i, row])] for i in range(live)], axis=axis)

    def weigh(p, rel):
        head = pieces[p][0]
        queries = jnp.concatenate(
            [qbuf[head, rel, :, r * HD:(r + 1) * HD] for r in range(share)], axis=0
        )
        scores = lax.dot_general(
            queries, picked(p, rel), (((1,), (1,)), ((), ())),
            preferred_element_type=jnp.float32,
        )
        row_max = jnp.max(scores, axis=1, keepdims=True)
        weights = jnp.exp2((scores - row_max) * factor)
        total = jnp.sum(weights, axis=1, keepdims=True)
        lbuf[rel] = jnp.broadcast_to(total, lbuf.shape[1:])
        pbuf[rel] = weights.astype(jnp.bfloat16)

    def lanes(p):
        head, kind, low, size = pieces[p]
        return pl.ds(low * share, size * share)

    def back(p, rel):
        head, kind, low, size = pieces[p]
        start = pl.multiple_of((chip * heads + head) * width, width) + low * share
        dst = o_ref.at[:, pl.ds(pl.multiple_of(start, HD), size * share)]
        src = obuf.at[head, rel, :, lanes(p)]
        return pltpu.make_async_remote_copy(
            src, dst, o_send.at[p, rel], o_recv.at[p, rel],
            device_id=device(column, partner(chip, rel), core), device_id_type=MESH,
        )

    def keep(head, p):
        return pltpu.make_async_copy(obuf.at[head, 0], o_ref.at[:, cols(chip * heads + head, width)], o_send.at[p, 0])

    def attend(p, rel):
        head, kind, low, size = pieces[p]
        dims = (((1,), (1 if p in turned else 0,)), ((), ()))
        product = lax.dot_general(pbuf[rel], picked(p, rel), dims, preferred_element_type=jnp.float32)
        result = (product / lbuf[rel][:, :size]).astype(jnp.bfloat16)
        rows = result.shape[0] // share
        obuf[head, rel, :, lanes(p)] = jnp.concatenate(
            [result[r * rows:(r + 1) * rows] for r in range(share)], axis=1
        )

        @pl.when(rel > 0)
        def _():
            back(p, rel).start()

        if p not in turned:
            @pl.when(rel == 0)
            def _():
                keep(head, p).start()

    def in_order(packed):
        parts = [pieces[p][2:] for p in turned]
        return jnp.concatenate([
            packed[:, low * share + r * size:low * share + (r + 1) * size]
            for r in range(share) for low, size in parts
        ], axis=1)

    def ready(p):
        crossed(p)
        head, kind = pieces[p][:2]
        if kind == 0:
            own(count + head).wait()
            for rel in range(1, CHIPS):
                plane(count + head, rel).wait_recv()

    def unit(p, step):
        if pieces[p][1] == 0:
            weigh(p, step)
        else:
            attend(p, CHIPS - 1 - step)

    for p in straight:
        leave_both(p, 0)
        for rel in range(1, CHIPS):
            plane(p, rel).start()
    for head in range(heads - 1):
        for rel in range(1, CHIPS):
            plane(count + head, rel).start()
    for rel in range(CHIPS):
        take(rel).wait()
        vturn[rel] = vin[rel].T
    for p in turned:
        own(p).start()
        for rel in range(1, CHIPS):
            plane(p, rel).start()
    for rel in range(1, CHIPS):
        plane(count + heads - 1, rel).start()
    first(0)
    for p in turned:
        leave_both(p, 0)
    fetch.wait()
    for p in range(count):
        if p + 1 < count:
            first(p + 1)
        if p > 0:
            ready(p - 1)

        @pl.loop(0, CHIPS)
        def _(step):
            if p > 0:
                unit(p - 1, step)
            relay(p, step)

        if lay.columns > CHIPS:
            @pl.loop(CHIPS, lay.columns)
            def _(step):
                relay(p, step)

    ready(count - 1)

    @pl.loop(0, CHIPS)
    def _(step):
        unit(count - 1, step)

    mine = cols(chip * heads + heads - 1, width)
    o_ref[:, mine] = in_order(obuf[heads - 1, 0])

    for item in range(count + heads):
        for rel in range(1, CHIPS):
            plane(item, rel).wait_send()

    @pl.loop(0, lay.columns)
    def _(col):
        for p in range(count):
            @pl.when((col >= column) & has_down)
            def _():
                hop(p, 0, col).wait_send()

            @pl.when((col <= column) & has_up)
            def _():
                hop(p, 1, col).wait_send()

            cross(p, col, core).wait_send()

    for p in range(count):
        head, kind = pieces[p][:2]
        if kind == 1 and p not in turned:
            keep(head, p).wait()
            for rel in range(1, CHIPS):
                back(p, rel).wait()
    for rel in range(1, CHIPS):
        for p in turned:
            back(p, rel).wait()
        theirs = cols(partner(chip, rel) * heads + heads - 1, width)
        o_ref[:, theirs] = in_order(o_ref[:, theirs])


def hand_out(src, dst, sem):
    parts = sem.shape[0]
    rows = src.shape[0] // parts
    copies = [
        pltpu.make_async_copy(src.at[pl.ds(i * rows, rows)], dst.at[pl.ds(i * rows, rows)], sem.at[i])
        for i in range(parts)
    ]
    for copy in copies:
        copy.start()
    for copy in copies:
        copy.wait()


def solution(mesh):
    lay = Layout(mesh.shape["uly"], mesh.shape["blk"])

    def body(queries, keys, values, live_blocks):
        rows, hidden = queries.shape
        heads = keys.shape[1] // HD // CHIPS
        width = hidden // CHIPS // heads
        share = width // HD
        slots = lay.columns * GROUP
        count = len(cut(heads))
        keys_seen = live_blocks.shape[1] * rows
        bf16, f32 = jnp.bfloat16, jnp.float32
        dma = pltpu.SemaphoreType.DMA

        def call(*refs):
            kernel(lay, *refs)

        held = pl.pallas_call(
            call,
            out_shape=pltpu.VMEM((rows, hidden), bf16),
            in_specs=[pl.BlockSpec(memory_space=pltpu.HBM)] * 4,
            out_specs=pl.BlockSpec(memory_space=pltpu.VMEM),
            scratch_shapes=[
                pltpu.SMEM(live_blocks.shape[::-1], live_blocks.dtype),
                dma,
                pltpu.VMEM((heads, CHIPS, rows, width), bf16),
                [
                    pltpu.VMEM((slots, *((p[3], rows) if turns(p, heads) else (rows, HD))), bf16)
                    for p in cut(heads)
                ],
                *[pltpu.VMEM((CHIPS, rows, HD), bf16) for _ in range(2)],
                pltpu.VMEM((CHIPS, rows * share, keys_seen), bf16),
                pltpu.VMEM((CHIPS, rows * share, HD), f32),
                pltpu.VMEM((heads, CHIPS, rows, width), bf16),
                dma((count + heads, CHIPS)),
                dma((count + heads, CHIPS)),
                dma((count + heads,)),
                dma((CHIPS,)),
                dma((count, 2, lay.columns)),
                dma((count, lay.columns)),
                dma((count, lay.columns)),
                dma((count, lay.columns)),
                dma((count, CHIPS)),
                dma((count, CHIPS)),
            ],
            compiler_params=pltpu.CompilerParams(
                collective_id=0, has_side_effects=True, vmem_limit_bytes=59 * 2**20
            ),
            name="group_attention",
        )(live_blocks.T, queries, keys, values)
        return pl.pallas_call(
            hand_out,
            out_shape=jax.ShapeDtypeStruct((rows, hidden), bf16),
            in_specs=[pl.BlockSpec(memory_space=pl.ANY)],
            out_specs=pl.BlockSpec(memory_space=pl.ANY),
            scratch_shapes=[dma((8,))],
            compiler_params=pltpu.CompilerParams(vmem_limit_bytes=2**20),
            name="hand_out",
        )(held)

    spec = P(("blk", "uly"), None)
    return jax.shard_map(
        body, mesh=mesh, in_specs=(spec, spec, spec, P()), out_specs=spec, check_vma=False
    )
```

```python
import math

import jax
import jax.numpy as jnp
from jax import lax
from jax.experimental import pallas as pl
from jax.experimental.pallas import tpu as pltpu
from jax.sharding import PartitionSpec as P

HD = 128
CORES = 2
SIDE = 2
CHIPS = SIDE * SIDE
GROUP = CHIPS * CORES
MESH = pl.DeviceIdType.MESH


class Layout:
    def __init__(self, n_uly, n_blk):
        self.n_uly = n_uly
        self.nx = n_blk // CORES
        self.ny = 2 ** (int(math.log2(n_uly)) // 2)
        self.nz = n_uly // self.ny
        self.columns = n_uly * n_blk // GROUP

    def split(self, uly, blk):
        x, core = blk // CORES, blk % CORES
        z, y = uly // self.ny, uly % self.ny
        column = ((x // SIDE) * (self.ny // SIDE) + y // SIDE) * self.nz + z
        return column, (x % SIDE) * SIDE + y % SIDE, core

    def join(self, column, chip, core):
        z, square = column % self.nz, column // self.nz
        x = (square // (self.ny // SIDE)) * SIDE + chip // SIDE
        y = (square % (self.ny // SIDE)) * SIDE + chip % SIDE
        return z * self.ny + y, x * CORES + core

    def slot(self, block):
        column, chip, core = self.split(block % self.n_uly, block // self.n_uly)
        return column * GROUP + core * CHIPS + chip


def partner(chip, rel):
    a = (chip // 2 + rel // 2) % 2
    b = (chip % 2 + rel % 2) % 2
    return a * 2 + b


def cut(heads):
    pieces = []
    for head in range(heads - 1):
        pieces += [(head, 0, 0, HD), (head, 1, 0, HD)]
    pieces.append((heads - 1, 0, 0, HD))
    low = 0
    for size in (3 * HD // 4, HD // 4):
        pieces.append((heads - 1, 1, low, size))
        low += size
    return pieces


def turns(piece, heads):
    return piece[0] == heads - 1 and piece[1] == 1


def kernel(lay, live_hbm, q_ref, k_ref, v_ref, o_ref,
           live_ref, live_sem, qbuf, bufs, vin, vturn, pbuf, lbuf, obuf,
           plane_send, plane_recv, own_sem, in_sem, z_send, z_recv, c_send, c_recv, o_send, o_recv):
    heads = k_ref.shape[1] // HD // CHIPS
    width = q_ref.shape[1] // CHIPS // heads
    share = width // HD
    live = live_ref.shape[0]
    last = lay.columns - 1
    pieces = cut(heads)
    count = len(pieces)
    turned = [p for p in range(count) if turns(pieces[p], heads)]
    column, chip, core = lay.split(lax.axis_index("uly"), lax.axis_index("blk"))

    def device(col, which, core_of):
        uly, blk = lay.join(col, which, core_of)
        return {"uly": uly, "blk": blk}

    has_down, has_up = column > 0, column < last
    middle = has_down & has_up
    down, up = jnp.maximum(column - 1, 0), jnp.minimum(column + 1, last)
    skips = ((column == 0) & (last > 1), jnp.minimum(column + 2, last)), ((column == last) & (last > 1), jnp.maximum(column - 2, 0))
    skipped = ((column == 2, jnp.maximum(column - 2, 0)), (column == last - 2, jnp.minimum(column + 2, last)))
    beyond = jnp.where(column == 0, skips[0][1], skips[1][1])
    targets = (
        device(down, chip, core), device(up, chip, core), device(beyond, chip, core), device(column, chip, 1 - core)
    )

    barrier = pltpu.get_barrier_semaphore()
    for rel in range(1, CHIPS):
        pl.semaphore_signal(
            barrier, inc=1, device_id=device(column, partner(chip, rel), core), device_id_type=MESH
        )
    pl.semaphore_signal(barrier, inc=1, device_id=targets[3], device_id_type=MESH)

    @pl.when(has_down)
    def _():
        pl.semaphore_signal(barrier, inc=1, device_id=targets[0], device_id_type=MESH)

    @pl.when(has_up)
    def _():
        pl.semaphore_signal(barrier, inc=1, device_id=targets[1], device_id_type=MESH)

    greeted = CHIPS + has_down.astype(jnp.int32) + has_up.astype(jnp.int32)
    for near, col in (*skips, *skipped):
        greeted = greeted + near.astype(jnp.int32)

        @pl.when(near)
        def _():
            pl.semaphore_signal(barrier, inc=1, device_id=device(col, chip, core), device_id_type=MESH)

    def cols(index, size):
        return pl.ds(pl.multiple_of(index * size, size), size)

    def slot_of(col, item, core_of):
        return col * GROUP + core_of * CHIPS + item

    here = slot_of(column, chip, core)

    def route(item, rel):
        if item >= count:
            head = item - count
            src = q_ref.at[:, cols(partner(chip, rel) * heads + head, width)]
            return src, qbuf.at[head, rel]
        head, kind, low, size = pieces[item]
        if item in turned:
            return vturn.at[rel, pl.ds(low, size)], bufs[item].at[here]
        src = (k_ref, v_ref)[kind].at[:, cols(partner(chip, rel) * heads + head, HD)]
        return src, bufs[item].at[here]

    def own(item):
        src, dst = route(item, 0)
        return pltpu.make_async_copy(src, dst, own_sem.at[item])

    def plane(item, rel):
        src, dst = route(item, rel)
        return pltpu.make_async_remote_copy(
            src, dst, plane_send.at[item, rel], plane_recv.at[item, rel],
            device_id=device(column, partner(chip, rel), core), device_id_type=MESH,
        )

    def take(rel):
        src = v_ref.at[:, cols(partner(chip, rel) * heads + heads - 1, HD)]
        return pltpu.make_async_copy(src, vin.at[rel], in_sem.at[rel])

    straight = [p for p in range(count) if p not in turned]

    fetch = pltpu.make_async_copy(live_hbm, live_ref, live_sem)
    for rel in range(CHIPS):
        take(rel).start()
    for item in (*straight, *range(count, count + heads)):
        own(item).start()
    fetch.start()
    pl.semaphore_wait(barrier, greeted)

    def chunk(p, col, core_of):
        return bufs[p].at[pl.ds(slot_of(col, 0, core_of), CHIPS)]

    def hop(p, way, col):
        ref = chunk(p, col, core)
        return pltpu.make_async_remote_copy(
            ref, ref, z_send.at[p, way, col], z_recv.at[p, col],
            device_id=targets[way], device_id_type=MESH,
        )

    def cross(p, col, core_of):
        ref = chunk(p, col, core_of)
        return pltpu.make_async_remote_copy(
            ref, ref, c_send.at[p, col], c_recv.at[p, col],
            device_id=targets[3], device_id_type=MESH,
        )

    def leave(p, way, rel):
        ref = bufs[p].at[slot_of(column, partner(chip, rel), core)]
        src = route(p, 0)[0] if rel == 0 else ref
        return pltpu.make_async_remote_copy(
            src, ref, z_send.at[p, way, column], z_recv.at[p, column],
            device_id=targets[way], device_id_type=MESH,
        )

    def leave_both(p, rel):
        @pl.when(has_down)
        def _():
            leave(p, 0, rel).start()

        @pl.when(has_up)
        def _():
            leave(p, 1, rel).start()

        if lay.columns > 2:
            @pl.when((column == 0) | (column == last))
            def _():
                leave(p, 2, rel).start()

    def first(p):
        if p > 0:
            leave_both(p, 0)
        for rel in range(1, CHIPS):
            plane(p, rel).wait_recv()
            leave_both(p, rel)
        own(p).wait()
        cross(p, column, core).start()

    def forwards_up(col):
        return has_up & jnp.logical_not((col == 0) & (column == 1))

    def forwards_down(col):
        return has_down & jnp.logical_not((col == last) & (column == last - 1))

    def relay(p, step):
        above, below = column + step, column - step

        @pl.when(below >= 0)
        def _():
            hop(p, 1, below).wait_recv()

            @pl.when(forwards_up(below))
            def _():
                hop(p, 1, below).start()

            cross(p, below, core).start()

        @pl.when(above <= last)
        def _():
            hop(p, 0, above).wait_recv()

            @pl.when(forwards_down(above))
            def _():
                hop(p, 0, above).start()

            cross(p, above, core).start()

    def relays(p):
        @pl.loop(1, lay.columns)
        def _(step):
            relay(p, step)

    def crossed(p):
        @pl.loop(0, lay.columns)
        def _(col):
            cross(p, col, 1 - core).wait_recv()

    factor = math.log2(math.e) / math.sqrt(HD)

    def picked(p, rel):
        uly, blk = lay.join(column, partner(chip, rel), core)
        row = blk * lay.n_uly + uly
        axis = 1 if p in turned else 0
        return jnp.concatenate([bufs[p][lay.slot(live_ref[i, row])] for i in range(live)], axis=axis)

    def weigh(p, rel):
        head = pieces[p][0]
        queries = jnp.concatenate(
            [qbuf[head, rel, :, r * HD:(r + 1) * HD] for r in range(share)], axis=0
        )
        scores = lax.dot_general(
            queries, picked(p, rel), (((1,), (1,)), ((), ())),
            preferred_element_type=jnp.float32,
        )
        row_max = jnp.max(scores, axis=1, keepdims=True)
        weights = jnp.exp2((scores - row_max) * factor)
        total = jnp.sum(weights, axis=1, keepdims=True)
        lbuf[rel] = jnp.broadcast_to(total, lbuf.shape[1:])
        pbuf[rel] = weights.astype(jnp.bfloat16)

    def lanes(p):
        head, kind, low, size = pieces[p]
        return pl.ds(low * share, size * share)

    def back(p, rel):
        head, kind, low, size = pieces[p]
        start = pl.multiple_of((chip * heads + head) * width, width) + low * share
        dst = o_ref.at[:, pl.ds(pl.multiple_of(start, HD), size * share)]
        src = obuf.at[head, rel, :, lanes(p)]
        return pltpu.make_async_remote_copy(
            src, dst, o_send.at[p, rel], o_recv.at[p, rel],
            device_id=device(column, partner(chip, rel), core), device_id_type=MESH,
        )

    def keep(head, p):
        return pltpu.make_async_copy(obuf.at[head, 0], o_ref.at[:, cols(chip * heads + head, width)], o_send.at[p, 0])

    def attend(p, rel):
        head, kind, low, size = pieces[p]
        dims = (((1,), (1 if p in turned else 0,)), ((), ()))
        product = lax.dot_general(pbuf[rel], picked(p, rel), dims, preferred_element_type=jnp.float32)
        result = (product / lbuf[rel][:, :size]).astype(jnp.bfloat16)
        rows = result.shape[0] // share
        obuf[head, rel, :, lanes(p)] = jnp.concatenate(
            [result[r * rows:(r + 1) * rows] for r in range(share)], axis=1
        )

        @pl.when(rel > 0)
        def _():
            back(p, rel).start()

        if p not in turned:
            @pl.when(rel == 0)
            def _():
                keep(head, p).start()

    def in_order(packed):
        parts = [pieces[p][2:] for p in turned]
        return jnp.concatenate([
            packed[:, low * share + r * size:low * share + (r + 1) * size]
            for r in range(share) for low, size in parts
        ], axis=1)

    def ready(p):
        crossed(p)
        head, kind = pieces[p][:2]
        if kind == 0:
            own(count + head).wait()
            for rel in range(1, CHIPS):
                plane(count + head, rel).wait_recv()

    def units(p):
        @pl.loop(0, CHIPS)
        def _(step):
            if pieces[p][1] == 0:
                weigh(p, step)
            else:
                attend(p, CHIPS - 1 - step)

    def settle(done, items):
        for item in items:
            for rel in range(1, CHIPS):
                plane(item, rel).wait_send()

        @pl.loop(0, lay.columns)
        def _(col):
            for p in done:
                @pl.when((col >= column) & forwards_down(col))
                def _():
                    hop(p, 0, col).wait_send()

                @pl.when((col <= column) & forwards_up(col))
                def _():
                    hop(p, 1, col).wait_send()

                if lay.columns > 2:
                    @pl.when((col == column) & ((column == 0) | (column == last)))
                    def _():
                        hop(p, 2, col).wait_send()

                cross(p, col, core).wait_send()

    leave_both(0, 0)
    for p in straight:
        for rel in range(1, CHIPS):
            plane(p, rel).start()
    for rel in range(CHIPS):
        take(rel).wait()
        vturn[rel] = vin[rel].T
    for p in turned:
        own(p).start()
        for rel in range(1, CHIPS):
            plane(p, rel).start()
    for head in range(heads):
        for rel in range(1, CHIPS):
            plane(count + head, rel).start()
    first(0)
    fetch.wait()

    @pl.when(jnp.logical_not(middle))
    def _():
        for p in range(1, count):
            first(p)

    for p in range(count):
        @pl.when(middle)
        def _():
            if p == 0:
                first(1)
            relays(p)
            if 0 < p < count - 1:
                first(p + 1)

        if p > 0:
            ready(p - 1)
            units(p - 1)

        @pl.when(jnp.logical_not(middle))
        def _():
            relays(p)

    ready(count - 1)
    units(count - 1)

    mine = cols(chip * heads + heads - 1, width)
    o_ref[:, mine] = in_order(obuf[heads - 1, 0])

    settle(range(count), range(count + heads))

    for p in range(count):
        head, kind = pieces[p][:2]
        if kind == 1 and p not in turned:
            keep(head, p).wait()
            for rel in range(1, CHIPS):
                back(p, rel).wait()
    for rel in range(1, CHIPS):
        for p in turned:
            back(p, rel).wait()
        theirs = cols(partner(chip, rel) * heads + heads - 1, width)
        o_ref[:, theirs] = in_order(o_ref[:, theirs])


def hand_out(src, dst, sem):
    parts = sem.shape[0]
    rows = src.shape[0] // parts
    copies = [
        pltpu.make_async_copy(src.at[pl.ds(i * rows, rows)], dst.at[pl.ds(i * rows, rows)], sem.at[i])
        for i in range(parts)
    ]
    for copy in copies:
        copy.start()
    for copy in copies:
        copy.wait()


def solution(mesh):
    lay = Layout(mesh.shape["uly"], mesh.shape["blk"])

    def body(queries, keys, values, live_blocks):
        rows, hidden = queries.shape
        heads = keys.shape[1] // HD // CHIPS
        width = hidden // CHIPS // heads
        share = width // HD
        slots = lay.columns * GROUP
        count = len(cut(heads))
        keys_seen = live_blocks.shape[1] * rows
        bf16, f32 = jnp.bfloat16, jnp.float32
        dma = pltpu.SemaphoreType.DMA

        def call(*refs):
            kernel(lay, *refs)

        held = pl.pallas_call(
            call,
            out_shape=pltpu.VMEM((rows, hidden), bf16),
            in_specs=[pl.BlockSpec(memory_space=pltpu.HBM)] * 4,
            out_specs=pl.BlockSpec(memory_space=pltpu.VMEM),
            scratch_shapes=[
                pltpu.SMEM(live_blocks.shape[::-1], live_blocks.dtype),
                dma,
                pltpu.VMEM((heads, CHIPS, rows, width), bf16),
                [
                    pltpu.VMEM((slots, *((p[3], rows) if turns(p, heads) else (rows, HD))), bf16)
                    for p in cut(heads)
                ],
                *[pltpu.VMEM((CHIPS, rows, HD), bf16) for _ in range(2)],
                pltpu.VMEM((CHIPS, rows * share, keys_seen), bf16),
                pltpu.VMEM((CHIPS, rows * share, HD), f32),
                pltpu.VMEM((heads, CHIPS, rows, width), bf16),
                dma((count + heads, CHIPS)),
                dma((count + heads, CHIPS)),
                dma((count + heads,)),
                dma((CHIPS,)),
                dma((count, 3, lay.columns)),
                dma((count, lay.columns)),
                dma((count, lay.columns)),
                dma((count, lay.columns)),
                dma((count, CHIPS)),
                dma((count, CHIPS)),
            ],
            compiler_params=pltpu.CompilerParams(
                collective_id=0, has_side_effects=True, vmem_limit_bytes=59 * 2**20
            ),
            name="group_attention",
        )(live_blocks.T, queries, keys, values)
        return pl.pallas_call(
            hand_out,
            out_shape=jax.ShapeDtypeStruct((rows, hidden), bf16),
            in_specs=[pl.BlockSpec(memory_space=pl.ANY)],
            out_specs=pl.BlockSpec(memory_space=pl.ANY),
            scratch_shapes=[dma((8,))],
            compiler_params=pltpu.CompilerParams(vmem_limit_bytes=2**20),
            name="hand_out",
        )(held)

    spec = P(("blk", "uly"), None)
    return jax.shard_map(
        body, mesh=mesh, in_specs=(spec, spec, spec, P()), out_specs=spec, check_vma=False
    )
```

```python
import math

import jax
import jax.numpy as jnp
from jax import lax
from jax.experimental import pallas as pl
from jax.experimental.pallas import tpu as pltpu
from jax.sharding import PartitionSpec as P

HD = 128
CORES = 2
SIDE = 2
CHIPS = SIDE * SIDE
GROUP = CHIPS * CORES
MESH = pl.DeviceIdType.MESH


class Layout:
    def __init__(self, n_uly, n_blk):
        self.n_uly = n_uly
        self.nx = n_blk // CORES
        self.ny = 2 ** (int(math.log2(n_uly)) // 2)
        self.nz = n_uly // self.ny
        self.columns = n_uly * n_blk // GROUP

    def split(self, uly, blk):
        x, core = blk // CORES, blk % CORES
        z, y = uly // self.ny, uly % self.ny
        column = ((x // SIDE) * (self.ny // SIDE) + y // SIDE) * self.nz + z
        return column, (x % SIDE) * SIDE + y % SIDE, core

    def join(self, column, chip, core):
        z, square = column % self.nz, column // self.nz
        x = (square // (self.ny // SIDE)) * SIDE + chip // SIDE
        y = (square % (self.ny // SIDE)) * SIDE + chip % SIDE
        return z * self.ny + y, x * CORES + core

    def slot(self, block):
        column, chip, core = self.split(block % self.n_uly, block // self.n_uly)
        return column * GROUP + core * CHIPS + chip


def partner(chip, rel):
    a = (chip // 2 + rel // 2) % 2
    b = (chip % 2 + rel % 2) % 2
    return a * 2 + b


def cut(heads):
    pieces = []
    for head in range(heads - 1):
        pieces += [(head, 0, 0, HD), (head, 1, 0, HD)]
    pieces.append((heads - 1, 0, 0, HD))
    low = 0
    for size in (3 * HD // 4, HD // 4):
        pieces.append((heads - 1, 1, low, size))
        low += size
    return pieces


def turns(piece, heads):
    return piece[0] == heads - 1 and piece[1] == 1


def kernel(lay, live_hbm, q_ref, k_ref, v_ref, o_ref,
           live_ref, live_sem, qbuf, bufs, vin, vturn, pbuf, lbuf, obuf,
           plane_send, plane_recv, own_sem, in_sem, z_send, z_recv, c_send, c_recv, o_send, o_recv, pace):
    heads = k_ref.shape[1] // HD // CHIPS
    width = q_ref.shape[1] // CHIPS // heads
    share = width // HD
    live = live_ref.shape[0]
    last = lay.columns - 1
    pieces = cut(heads)
    count = len(pieces)
    turned = [p for p in range(count) if turns(pieces[p], heads)]
    column, chip, core = lay.split(lax.axis_index("uly"), lax.axis_index("blk"))

    def device(col, which, core_of):
        uly, blk = lay.join(col, which, core_of)
        return {"uly": uly, "blk": blk}

    has_down, has_up = column > 0, column < last
    middle = has_down & has_up
    down, up = jnp.maximum(column - 1, 0), jnp.minimum(column + 1, last)
    skips = ((column == 0) & (last > 1), jnp.minimum(column + 2, last)), ((column == last) & (last > 1), jnp.maximum(column - 2, 0))
    skipped = ((column == 2, jnp.maximum(column - 2, 0)), (column == last - 2, jnp.minimum(column + 2, last)))
    beyond = jnp.where(column == 0, skips[0][1], skips[1][1])
    targets = (
        device(down, chip, core), device(up, chip, core), device(beyond, chip, core), device(column, chip, 1 - core)
    )

    barrier = pltpu.get_barrier_semaphore()
    for rel in range(1, CHIPS):
        pl.semaphore_signal(
            barrier, inc=1, device_id=device(column, partner(chip, rel), core), device_id_type=MESH
        )
    pl.semaphore_signal(barrier, inc=1, device_id=targets[3], device_id_type=MESH)

    @pl.when(has_down)
    def _():
        pl.semaphore_signal(barrier, inc=1, device_id=targets[0], device_id_type=MESH)

    @pl.when(has_up)
    def _():
        pl.semaphore_signal(barrier, inc=1, device_id=targets[1], device_id_type=MESH)

    greeted = CHIPS + has_down.astype(jnp.int32) + has_up.astype(jnp.int32)
    for near, col in (*skips, *skipped):
        greeted = greeted + near.astype(jnp.int32)

        @pl.when(near)
        def _():
            pl.semaphore_signal(barrier, inc=1, device_id=device(col, chip, core), device_id_type=MESH)

    def cols(index, size):
        return pl.ds(pl.multiple_of(index * size, size), size)

    def slot_of(col, item, core_of):
        return col * GROUP + core_of * CHIPS + item

    here = slot_of(column, chip, core)

    def route(item, rel):
        if item >= count:
            head = item - count
            src = q_ref.at[:, cols(partner(chip, rel) * heads + head, width)]
            return src, qbuf.at[head, rel]
        head, kind, low, size = pieces[item]
        if item in turned:
            return vturn.at[rel, pl.ds(low, size)], bufs[item].at[here]
        src = (k_ref, v_ref)[kind].at[:, cols(partner(chip, rel) * heads + head, HD)]
        return src, bufs[item].at[here]

    def own(item):
        src, dst = route(item, 0)
        return pltpu.make_async_copy(src, dst, own_sem.at[item])

    def plane(item, rel):
        src, dst = route(item, rel)
        return pltpu.make_async_remote_copy(
            src, dst, plane_send.at[item], plane_recv.at[item, rel],
            device_id=device(column, partner(chip, rel), core), device_id_type=MESH,
        )

    def take(rel):
        src = v_ref.at[:, cols(partner(chip, rel) * heads + heads - 1, HD)]
        return pltpu.make_async_copy(src, vin.at[rel], in_sem.at[rel])

    straight = [p for p in range(count) if p not in turned]

    fetch = pltpu.make_async_copy(live_hbm, live_ref, live_sem)
    for rel in range(CHIPS):
        take(rel).start()
    for item in (*straight, *range(count, count + heads)):
        own(item).start()
    fetch.start()
    pl.semaphore_wait(barrier, greeted)

    def chunk(p, col, core_of):
        return bufs[p].at[pl.ds(slot_of(col, 0, core_of), CHIPS)]

    def hop(p, way, col):
        ref = chunk(p, col, core)
        return pltpu.make_async_remote_copy(
            ref, ref, z_send.at[p, way, col], z_recv.at[p, col],
            device_id=targets[way], device_id_type=MESH,
        )

    def cross(p, col, core_of):
        ref = chunk(p, col, core_of)
        return pltpu.make_async_remote_copy(
            ref, ref, c_send.at[p], c_recv.at[p],
            device_id=targets[3], device_id_type=MESH,
        )

    def leave(p, way, rel):
        ref = bufs[p].at[slot_of(column, partner(chip, rel), core)]
        src = route(p, 0)[0] if rel == 0 else ref
        return pltpu.make_async_remote_copy(
            src, ref, z_send.at[p, way, column], z_recv.at[p, column],
            device_id=targets[way], device_id_type=MESH,
        )

    def leave_both(p, rel):
        @pl.when(has_down)
        def _():
            leave(p, 0, rel).start()

        @pl.when(has_up)
        def _():
            leave(p, 1, rel).start()

        if lay.columns > 2:
            @pl.when((column == 0) | (column == last))
            def _():
                leave(p, 2, rel).start()

    def first(p):
        if p > 0:
            leave_both(p, 0)
        for rel in range(1, CHIPS):
            plane(p, rel).wait_recv()
            leave_both(p, rel)
        own(p).wait()
        cross(p, column, core).start()

    def forwards_up(col):
        return has_up & jnp.logical_not((col == 0) & (column == 1))

    def forwards_down(col):
        return has_down & jnp.logical_not((col == last) & (column == last - 1))

    def relay(p, step):
        above, below = column + step, column - step

        @pl.when(below >= 0)
        def _():
            hop(p, 1, below).wait_recv()

            @pl.when(forwards_up(below))
            def _():
                hop(p, 1, below).start()

            cross(p, below, core).start()

        @pl.when(above <= last)
        def _():
            hop(p, 0, above).wait_recv()

            @pl.when(forwards_down(above))
            def _():
                hop(p, 0, above).start()

            cross(p, above, core).start()

    def relays(p):
        @pl.loop(1, lay.columns)
        def _(step):
            relay(p, step)

    def bulk(ref, sem):
        return pltpu.make_async_copy(ref, ref, sem)

    def half(p):
        return bufs[p].at[pl.ds(0, lay.columns * CHIPS)]

    def crossed(p):
        bulk(half(p), c_recv.at[p]).wait()

    factor = math.log2(math.e) / math.sqrt(HD)

    def picked(p, rel):
        uly, blk = lay.join(column, partner(chip, rel), core)
        row = blk * lay.n_uly + uly
        axis = 1 if p in turned else 0
        return jnp.concatenate([bufs[p][lay.slot(live_ref[i, row])] for i in range(live)], axis=axis)

    def weigh(p, rel):
        head = pieces[p][0]
        keys = picked(p, rel)
        rows = qbuf.shape[2]
        for r in range(share):
            scores = lax.dot_general(
                qbuf[head, rel, :, r * HD:(r + 1) * HD], keys, (((1,), (1,)), ((), ())),
                preferred_element_type=jnp.float32,
            )
            row_max = jnp.max(scores, axis=1, keepdims=True)
            weights = jnp.exp2((scores - row_max) * factor)
            total = jnp.sum(weights, axis=1, keepdims=True)
            lbuf[rel, r * rows:(r + 1) * rows] = jnp.broadcast_to(1 / total, (rows, HD))
            pbuf[rel, r * rows:(r + 1) * rows] = weights.astype(jnp.bfloat16)

    def lanes(p):
        head, kind, low, size = pieces[p]
        return pl.ds(low * share, size * share)

    def back(p, rel):
        head, kind, low, size = pieces[p]
        start = pl.multiple_of((chip * heads + head) * width, width) + low * share
        dst = o_ref.at[:, pl.ds(pl.multiple_of(start, HD), size * share)]
        src = obuf.at[head, rel, :, lanes(p)]
        return pltpu.make_async_remote_copy(
            src, dst, o_send.at[p], o_recv.at[p, rel],
            device_id=device(column, partner(chip, rel), core), device_id_type=MESH,
        )

    def keep(head, p):
        return pltpu.make_async_copy(obuf.at[head, 0], o_ref.at[:, cols(chip * heads + head, width)], o_recv.at[p, 0])

    def attend(p, rel):
        head, kind, low, size = pieces[p]
        dims = (((1,), (1 if p in turned else 0,)), ((), ()))
        product = lax.dot_general(pbuf[rel], picked(p, rel), dims, preferred_element_type=jnp.float32)
        result = (product * lbuf[rel][:, :size]).astype(jnp.bfloat16)
        rows = result.shape[0] // share
        obuf[head, rel, :, lanes(p)] = jnp.concatenate(
            [result[r * rows:(r + 1) * rows] for r in range(share)], axis=1
        )

        @pl.when(rel > 0)
        def _():
            back(p, rel).start()

        if p not in turned:
            @pl.when(rel == 0)
            def _():
                keep(head, p).start()

    def in_order(packed):
        parts = [pieces[p][2:] for p in turned]
        return jnp.concatenate([
            packed[:, low * share + r * size:low * share + (r + 1) * size]
            for r in range(share) for low, size in parts
        ], axis=1)

    def ready(p):
        crossed(p)
        head, kind = pieces[p][:2]
        if kind == 0:
            own(count + head).wait()
            for rel in range(1, CHIPS):
                plane(count + head, rel).wait_recv()

    def units(p, coming=None):
        @pl.loop(0, CHIPS)
        def _(step):
            if p >= 0 and pieces[p][1] == 0:
                weigh(p, step)
            elif p >= 0:
                attend(p, CHIPS - 1 - step)
            if coming is not None:
                @pl.when((step > 0) & jnp.logical_not(middle))
                def _():
                    relay(coming, step)

        if coming is not None and lay.columns > CHIPS:
            @pl.when(jnp.logical_not(middle))
            def _():
                @pl.loop(CHIPS, lay.columns)
                def _(step):
                    relay(coming, step)

    def gone(p):
        @pl.loop(0, lay.columns)
        def _(col):
            @pl.when((col >= column) & forwards_down(col))
            def _():
                hop(p, 0, col).wait_send()

            @pl.when((col <= column) & forwards_up(col))
            def _():
                hop(p, 1, col).wait_send()

    paced = range(turned[0] - 2, count - 2)

    def keep_pace(p):
        gone(p)
        pl.semaphore_signal(pace, inc=1, device_id=targets[3], device_id_type=MESH)
        pl.semaphore_wait(pace, 1)

    def settle():
        for item in range(count + heads):
            ref = bufs[item].at[pl.ds(0, CHIPS - 1)] if item < count else qbuf.at[0, pl.ds(0, CHIPS - 1)]
            bulk(ref, plane_send.at[item]).wait()
        for p in range(count):
            bulk(half(p), c_send.at[p]).wait()

        @pl.when(middle)
        def _():
            for p in range(count):
                if p not in paced:
                    gone(p)

        @pl.when(jnp.logical_not(middle))
        def _():
            for p in range(count):
                @pl.when(has_down)
                def _():
                    hop(p, 0, column).wait_send()

                @pl.when(has_up)
                def _():
                    hop(p, 1, column).wait_send()

                if lay.columns > 2:
                    hop(p, 2, column).wait_send()

    leave_both(0, 0)
    for p in straight:
        for rel in range(1, CHIPS):
            plane(p, rel).start()
    for rel in range(CHIPS):
        take(rel).wait()
        vturn[rel] = vin[rel].T
    for p in turned:
        own(p).start()
        for rel in range(1, CHIPS):
            plane(p, rel).start()
    for head in range(heads):
        for rel in range(1, CHIPS):
            plane(count + head, rel).start()
    first(0)
    fetch.wait()

    @pl.when(jnp.logical_not(middle))
    def _():
        for p in range(1, count):
            first(p)

    for p in range(count):
        @pl.when(middle)
        def _():
            if p == 0:
                first(1)
            relays(p)
            if 0 < p < count - 1:
                if p - 1 in paced:
                    keep_pace(p - 1)
                first(p + 1)

        if p > 0:
            ready(p - 1)
        units(p - 1, p)

    ready(count - 1)
    units(count - 1)

    mine = cols(chip * heads + heads - 1, width)
    o_ref[:, mine] = in_order(obuf[heads - 1, 0])

    settle()

    for p in range(count):
        head, kind = pieces[p][:2]
        if kind == 1 and p not in turned:
            keep(head, p).wait()
            bulk(obuf.at[head, pl.ds(1, CHIPS - 1)], o_send.at[p]).wait()
            for rel in range(1, CHIPS):
                back(p, rel).wait_recv()
    for rel in range(1, CHIPS):
        for p in turned:
            back(p, rel).wait_recv()
        theirs = cols(partner(chip, rel) * heads + heads - 1, width)
        o_ref[:, theirs] = in_order(o_ref[:, theirs])
    for p in turned:
        bulk(obuf.at[heads - 1, pl.ds(1, CHIPS - 1), :, lanes(p)], o_send.at[p]).wait()


def hand_out(src, dst, sem):
    parts = sem.shape[0]
    rows = src.shape[0] // parts
    copies = [
        pltpu.make_async_copy(src.at[pl.ds(i * rows, rows)], dst.at[pl.ds(i * rows, rows)], sem.at[i])
        for i in range(parts)
    ]
    for copy in copies:
        copy.start()
    for copy in copies:
        copy.wait()


def solution(mesh):
    lay = Layout(mesh.shape["uly"], mesh.shape["blk"])

    def body(queries, keys, values, live_blocks):
        rows, hidden = queries.shape
        heads = keys.shape[1] // HD // CHIPS
        width = hidden // CHIPS // heads
        share = width // HD
        slots = lay.columns * GROUP
        count = len(cut(heads))
        keys_seen = live_blocks.shape[1] * rows
        bf16, f32 = jnp.bfloat16, jnp.float32
        dma = pltpu.SemaphoreType.DMA

        def call(*refs):
            kernel(lay, *refs)

        held = pl.pallas_call(
            call,
            out_shape=pltpu.VMEM((rows, hidden), bf16),
            in_specs=[pl.BlockSpec(memory_space=pltpu.HBM)] * 4,
            out_specs=pl.BlockSpec(memory_space=pltpu.VMEM),
            scratch_shapes=[
                pltpu.SMEM(live_blocks.shape[::-1], live_blocks.dtype),
                dma,
                pltpu.VMEM((heads, CHIPS, rows, width), bf16),
                [
                    pltpu.VMEM((slots, *((p[3], rows) if turns(p, heads) else (rows, HD))), bf16)
                    for p in cut(heads)
                ],
                *[pltpu.VMEM((CHIPS, rows, HD), bf16) for _ in range(2)],
                pltpu.VMEM((CHIPS, rows * share, keys_seen), bf16),
                pltpu.VMEM((CHIPS, rows * share, HD), f32),
                pltpu.VMEM((heads, CHIPS, rows, width), bf16),
                dma((count + heads,)),
                dma((count + heads, CHIPS)),
                dma((count + heads,)),
                dma((CHIPS,)),
                dma((count, 3, lay.columns)),
                dma((count, lay.columns)),
                dma((count,)),
                dma((count,)),
                dma((count,)),
                dma((count, CHIPS)),
                pltpu.SemaphoreType.REGULAR,
            ],
            compiler_params=pltpu.CompilerParams(
                collective_id=0, has_side_effects=True, vmem_limit_bytes=59 * 2**20
            ),
            name="group_attention",
        )(live_blocks.T, queries, keys, values)
        return pl.pallas_call(
            hand_out,
            out_shape=jax.ShapeDtypeStruct((rows, hidden), bf16),
            in_specs=[pl.BlockSpec(memory_space=pl.ANY)],
            out_specs=pl.BlockSpec(memory_space=pl.ANY),
            scratch_shapes=[dma((8,))],
            compiler_params=pltpu.CompilerParams(vmem_limit_bytes=2**20),
            name="hand_out",
        )(held)

    spec = P(("blk", "uly"), None)
    return jax.shard_map(
        body, mesh=mesh, in_specs=(spec, spec, spec, P()), out_specs=spec, check_vma=False
    )
```

```python
import math

import jax
import jax.numpy as jnp
from jax import lax
from jax.experimental import pallas as pl
from jax.experimental.pallas import tpu as pltpu
from jax.sharding import PartitionSpec as P

HD = 128
CORES = 2
SIDE = 2
CHIPS = SIDE * SIDE
GROUP = CHIPS * CORES
MESH = pl.DeviceIdType.MESH


class Layout:
    def __init__(self, n_uly, n_blk):
        self.n_uly = n_uly
        self.nx = n_blk // CORES
        self.ny = 2 ** (int(math.log2(n_uly)) // 2)
        self.nz = n_uly // self.ny
        self.columns = n_uly * n_blk // GROUP

    def split(self, uly, blk):
        x, core = blk // CORES, blk % CORES
        z, y = uly // self.ny, uly % self.ny
        column = ((x // SIDE) * (self.ny // SIDE) + y // SIDE) * self.nz + z
        return column, (x % SIDE) * SIDE + y % SIDE, core

    def join(self, column, chip, core):
        z, square = column % self.nz, column // self.nz
        x = (square // (self.ny // SIDE)) * SIDE + chip // SIDE
        y = (square % (self.ny // SIDE)) * SIDE + chip % SIDE
        return z * self.ny + y, x * CORES + core

    def slot(self, block):
        column, chip, core = self.split(block % self.n_uly, block // self.n_uly)
        return column * GROUP + core * CHIPS + chip


def partner(chip, rel):
    a = (chip // 2 + rel // 2) % 2
    b = (chip % 2 + rel % 2) % 2
    return a * 2 + b


def cut(heads):
    pieces = []
    for head in range(heads - 1):
        pieces += [(head, 0, 0, HD), (head, 1, 0, HD)]
    pieces.append((heads - 1, 0, 0, HD))
    low = 0
    for size in (HD // 2, HD // 2):
        pieces.append((heads - 1, 1, low, size))
        low += size
    return pieces


def turns(piece, heads):
    return piece[0] == heads - 1 and piece[1] == 1


def kernel(lay, live_hbm, q_ref, k_ref, v_ref, o_ref,
           live_ref, live_sem, qbuf, bufs, vin, vturn, pbuf, lbuf, obuf,
           plane_send, plane_recv, own_sem, in_sem, z_send, z_recv, c_send, c_recv, o_send, o_recv, pace):
    heads = k_ref.shape[1] // HD // CHIPS
    width = q_ref.shape[1] // CHIPS // heads
    share = width // HD
    live = live_ref.shape[0]
    last = lay.columns - 1
    pieces = cut(heads)
    count = len(pieces)
    turned = [p for p in range(count) if turns(pieces[p], heads)]
    column, chip, core = lay.split(lax.axis_index("uly"), lax.axis_index("blk"))

    def device(col, which, core_of):
        uly, blk = lay.join(col, which, core_of)
        return {"uly": uly, "blk": blk}

    has_down, has_up = column > 0, column < last
    middle = has_down & has_up
    down, up = jnp.maximum(column - 1, 0), jnp.minimum(column + 1, last)
    skips = ((column == 0) & (last > 1), jnp.minimum(column + 2, last)), ((column == last) & (last > 1), jnp.maximum(column - 2, 0))
    skipped = ((column == 2, jnp.maximum(column - 2, 0)), (column == last - 2, jnp.minimum(column + 2, last)))
    beyond = jnp.where(column == 0, skips[0][1], skips[1][1])
    targets = (
        device(down, chip, core), device(up, chip, core), device(beyond, chip, core), device(column, chip, 1 - core)
    )

    barrier = pltpu.get_barrier_semaphore()
    for rel in range(1, CHIPS):
        pl.semaphore_signal(
            barrier, inc=1, device_id=device(column, partner(chip, rel), core), device_id_type=MESH
        )
    pl.semaphore_signal(barrier, inc=1, device_id=targets[3], device_id_type=MESH)

    @pl.when(has_down)
    def _():
        pl.semaphore_signal(barrier, inc=1, device_id=targets[0], device_id_type=MESH)

    @pl.when(has_up)
    def _():
        pl.semaphore_signal(barrier, inc=1, device_id=targets[1], device_id_type=MESH)

    greeted = CHIPS + has_down.astype(jnp.int32) + has_up.astype(jnp.int32)
    for near, col in (*skips, *skipped):
        greeted = greeted + near.astype(jnp.int32)

        @pl.when(near)
        def _():
            pl.semaphore_signal(barrier, inc=1, device_id=device(col, chip, core), device_id_type=MESH)

    def cols(index, size):
        return pl.ds(pl.multiple_of(index * size, size), size)

    def slot_of(col, item, core_of):
        return col * GROUP + core_of * CHIPS + item

    here = slot_of(column, chip, core)

    def route(item, rel):
        if item >= count:
            head = item - count
            src = q_ref.at[:, cols(partner(chip, rel) * heads + head, width)]
            return src, qbuf.at[head, rel]
        head, kind, low, size = pieces[item]
        if item in turned:
            return vturn.at[rel, pl.ds(low, size)], bufs[item].at[here]
        src = (k_ref, v_ref)[kind].at[:, cols(partner(chip, rel) * heads + head, HD)]
        return src, bufs[item].at[here]

    def own(item):
        src, dst = route(item, 0)
        return pltpu.make_async_copy(src, dst, own_sem.at[item])

    def plane(item, rel):
        src, dst = route(item, rel)
        return pltpu.make_async_remote_copy(
            src, dst, plane_send.at[item], plane_recv.at[item, rel],
            device_id=device(column, partner(chip, rel), core), device_id_type=MESH,
        )

    def take(rel):
        src = v_ref.at[:, cols(partner(chip, rel) * heads + heads - 1, HD)]
        return pltpu.make_async_copy(src, vin.at[rel], in_sem.at[rel])

    straight = [p for p in range(count) if p not in turned]

    fetch = pltpu.make_async_copy(live_hbm, live_ref, live_sem)
    for rel in range(CHIPS):
        take(rel).start()
    for item in (*straight, *range(count, count + heads)):
        own(item).start()
    fetch.start()
    pl.semaphore_wait(barrier, greeted)

    def chunk(p, col, core_of):
        return bufs[p].at[pl.ds(slot_of(col, 0, core_of), CHIPS)]

    def hop(p, way, col):
        ref = chunk(p, col, core)
        return pltpu.make_async_remote_copy(
            ref, ref, z_send.at[p, way, col], z_recv.at[p, col],
            device_id=targets[way], device_id_type=MESH,
        )

    def cross(p, col, core_of):
        ref = chunk(p, col, core_of)
        return pltpu.make_async_remote_copy(
            ref, ref, c_send.at[p], c_recv.at[p],
            device_id=targets[3], device_id_type=MESH,
        )

    def leave(p, way, rel):
        ref = bufs[p].at[slot_of(column, partner(chip, rel), core)]
        src = route(p, 0)[0] if rel == 0 else ref
        return pltpu.make_async_remote_copy(
            src, ref, z_send.at[p, way, column], z_recv.at[p, column],
            device_id=targets[way], device_id_type=MESH,
        )

    def leave_both(p, rel):
        @pl.when(has_down)
        def _():
            leave(p, 0, rel).start()

        @pl.when(has_up)
        def _():
            leave(p, 1, rel).start()

        if lay.columns > 2:
            @pl.when((column == 0) | (column == last))
            def _():
                leave(p, 2, rel).start()

    def first(p):
        for rel in range(1, CHIPS):
            plane(p, rel).wait_recv()
            if p == 0:
                leave_both(p, rel)
        own(p).wait()
        if p > 0:
            @pl.when(has_down)
            def _():
                hop(p, 0, column).start()

            @pl.when(has_up)
            def _():
                hop(p, 1, column).start()

            if lay.columns > 2:
                @pl.when((column == 0) | (column == last))
                def _():
                    hop(p, 2, column).start()
        cross(p, column, core).start()

    def forwards_up(col):
        return has_up & jnp.logical_not((col == 0) & (column == 1))

    def forwards_down(col):
        return has_down & jnp.logical_not((col == last) & (column == last - 1))

    def relay(p, step):
        above, below = column + step, column - step

        @pl.when(below >= 0)
        def _():
            hop(p, 1, below).wait_recv()

            @pl.when(forwards_up(below))
            def _():
                hop(p, 1, below).start()

            cross(p, below, core).start()

        @pl.when(above <= last)
        def _():
            hop(p, 0, above).wait_recv()

            @pl.when(forwards_down(above))
            def _():
                hop(p, 0, above).start()

            cross(p, above, core).start()

    def relays(p):
        @pl.loop(1, lay.columns)
        def _(step):
            relay(p, step)

    def bulk(ref, sem):
        return pltpu.make_async_copy(ref, ref, sem)

    def half(p):
        return bufs[p].at[pl.ds(0, lay.columns * CHIPS)]

    def crossed(p):
        bulk(half(p), c_recv.at[p]).wait()

    factor = math.log2(math.e) / math.sqrt(HD)

    def picked(p, rel):
        uly, blk = lay.join(column, partner(chip, rel), core)
        row = blk * lay.n_uly + uly
        axis = 1 if p in turned else 0
        return jnp.concatenate([bufs[p][lay.slot(live_ref[i, row])] for i in range(live)], axis=axis)

    def weigh(p, rel):
        head = pieces[p][0]
        keys = picked(p, rel)
        rows = qbuf.shape[2]
        for r in range(share):
            scores = lax.dot_general(
                qbuf[head, rel, :, r * HD:(r + 1) * HD], keys, (((1,), (1,)), ((), ())),
                preferred_element_type=jnp.float32,
            )
            row_max = jnp.max(scores, axis=1, keepdims=True)
            weights = jnp.exp2((scores - row_max) * factor)
            total = jnp.sum(weights, axis=1, keepdims=True)
            lbuf[rel, r * rows:(r + 1) * rows] = jnp.broadcast_to(1 / total, (rows, HD))
            pbuf[rel, r * rows:(r + 1) * rows] = weights.astype(jnp.bfloat16)

    def lanes(p):
        head, kind, low, size = pieces[p]
        return pl.ds(low * share, size * share)

    def back(p, rel):
        head, kind, low, size = pieces[p]
        start = pl.multiple_of((chip * heads + head) * width, width) + low * share
        dst = o_ref.at[:, pl.ds(pl.multiple_of(start, HD), size * share)]
        src = obuf.at[head, rel, :, lanes(p)]
        return pltpu.make_async_remote_copy(
            src, dst, o_send.at[p], o_recv.at[p, rel],
            device_id=device(column, partner(chip, rel), core), device_id_type=MESH,
        )

    def keep(head, p):
        return pltpu.make_async_copy(obuf.at[head, 0], o_ref.at[:, cols(chip * heads + head, width)], o_recv.at[p, 0])

    def attend(p, rel):
        head, kind, low, size = pieces[p]
        dims = (((1,), (1 if p in turned else 0,)), ((), ()))
        product = lax.dot_general(pbuf[rel], picked(p, rel), dims, preferred_element_type=jnp.float32)
        result = (product * lbuf[rel][:, :size]).astype(jnp.bfloat16)
        rows = result.shape[0] // share
        obuf[head, rel, :, lanes(p)] = jnp.concatenate(
            [result[r * rows:(r + 1) * rows] for r in range(share)], axis=1
        )

        @pl.when(rel > 0)
        def _():
            back(p, rel).start()

        if p not in turned:
            @pl.when(rel == 0)
            def _():
                keep(head, p).start()

    def in_order(packed):
        parts = [pieces[p][2:] for p in turned]
        return jnp.concatenate([
            packed[:, low * share + r * size:low * share + (r + 1) * size]
            for r in range(share) for low, size in parts
        ], axis=1)

    def ready(p):
        crossed(p)
        head, kind = pieces[p][:2]
        if kind == 0:
            own(count + head).wait()
            for rel in range(1, CHIPS):
                plane(count + head, rel).wait_recv()

    def units(p, coming=None):
        @pl.loop(0, CHIPS)
        def _(step):
            if p >= 0 and pieces[p][1] == 0:
                weigh(p, step)
            elif p >= 0:
                attend(p, CHIPS - 1 - step)
            if coming is not None:
                @pl.when((step > 0) & jnp.logical_not(middle))
                def _():
                    relay(coming, step)

        if coming is not None and lay.columns > CHIPS:
            @pl.when(jnp.logical_not(middle))
            def _():
                @pl.loop(CHIPS, lay.columns)
                def _(step):
                    relay(coming, step)

    def gone(p):
        @pl.loop(0, lay.columns)
        def _(col):
            @pl.when((col >= column) & forwards_down(col))
            def _():
                hop(p, 0, col).wait_send()

            @pl.when((col <= column) & forwards_up(col))
            def _():
                hop(p, 1, col).wait_send()

    paced = range(turned[0] - 2, count - 2)

    def keep_pace(p):
        gone(p)
        pl.semaphore_signal(pace, inc=1, device_id=targets[3], device_id_type=MESH)
        pl.semaphore_wait(pace, 1)

    def settle():
        for item in range(count + heads):
            ref = bufs[item].at[pl.ds(0, CHIPS - 1)] if item < count else qbuf.at[0, pl.ds(0, CHIPS - 1)]
            bulk(ref, plane_send.at[item]).wait()
        for p in range(count):
            bulk(half(p), c_send.at[p]).wait()

        @pl.when(middle)
        def _():
            for p in range(count):
                if p not in paced:
                    gone(p)

        @pl.when(jnp.logical_not(middle))
        def _():
            for p in range(count):
                @pl.when(has_down)
                def _():
                    hop(p, 0, column).wait_send()

                @pl.when(has_up)
                def _():
                    hop(p, 1, column).wait_send()

                if lay.columns > 2:
                    hop(p, 2, column).wait_send()

    leave_both(0, 0)

    for p in straight:
        for rel in range(1, CHIPS):
            plane(p, rel).start()
    for rel in range(CHIPS):
        take(rel).wait()
        vturn[rel] = vin[rel].T
    for p in turned:
        own(p).start()
        for rel in range(1, CHIPS):
            plane(p, rel).start()
    for head in range(heads):
        for rel in range(1, CHIPS):
            plane(count + head, rel).start()
    first(0)
    fetch.wait()

    @pl.when(jnp.logical_not(middle))
    def _():
        for p in range(1, count):
            first(p)

    for p in range(count):
        @pl.when(middle)
        def _():
            if p == 0:
                first(1)
            relays(p)
            if 0 < p < count - 1:
                if p - 1 in paced:
                    keep_pace(p - 1)
                first(p + 1)

        if p > 0:
            ready(p - 1)
        units(p - 1, p)

    ready(count - 1)
    units(count - 1)

    mine = cols(chip * heads + heads - 1, width)
    o_ref[:, mine] = in_order(obuf[heads - 1, 0])

    settle()

    for p in range(count):
        head, kind = pieces[p][:2]
        if kind == 1 and p not in turned:
            keep(head, p).wait()
            bulk(obuf.at[head, pl.ds(1, CHIPS - 1)], o_send.at[p]).wait()
            for rel in range(1, CHIPS):
                back(p, rel).wait_recv()
    for rel in range(1, CHIPS):
        for p in turned:
            back(p, rel).wait_recv()
        theirs = cols(partner(chip, rel) * heads + heads - 1, width)
        o_ref[:, theirs] = in_order(o_ref[:, theirs])
    for p in turned:
        bulk(obuf.at[heads - 1, pl.ds(1, CHIPS - 1), :, lanes(p)], o_send.at[p]).wait()


def hand_out(src, dst, sem):
    parts = sem.shape[0]
    rows = src.shape[0] // parts
    copies = [
        pltpu.make_async_copy(src.at[pl.ds(i * rows, rows)], dst.at[pl.ds(i * rows, rows)], sem.at[i])
        for i in range(parts)
    ]
    for copy in copies:
        copy.start()
    for copy in copies:
        copy.wait()


def solution(mesh):
    lay = Layout(mesh.shape["uly"], mesh.shape["blk"])

    def body(queries, keys, values, live_blocks):
        rows, hidden = queries.shape
        heads = keys.shape[1] // HD // CHIPS
        width = hidden // CHIPS // heads
        share = width // HD
        slots = lay.columns * GROUP
        count = len(cut(heads))
        keys_seen = live_blocks.shape[1] * rows
        bf16, f32 = jnp.bfloat16, jnp.float32
        dma = pltpu.SemaphoreType.DMA

        def call(*refs):
            kernel(lay, *refs)

        held = pl.pallas_call(
            call,
            out_shape=pltpu.VMEM((rows, hidden), bf16),
            in_specs=[pl.BlockSpec(memory_space=pltpu.HBM)] * 4,
            out_specs=pl.BlockSpec(memory_space=pltpu.VMEM),
            scratch_shapes=[
                pltpu.SMEM(live_blocks.shape[::-1], live_blocks.dtype),
                dma,
                pltpu.VMEM((heads, CHIPS, rows, width), bf16),
                [
                    pltpu.VMEM((slots, *((p[3], rows) if turns(p, heads) else (rows, HD))), bf16)
                    for p in cut(heads)
                ],
                *[pltpu.VMEM((CHIPS, rows, HD), bf16) for _ in range(2)],
                pltpu.VMEM((CHIPS, rows * share, keys_seen), bf16),
                pltpu.VMEM((CHIPS, rows * share, HD), f32),
                pltpu.VMEM((heads, CHIPS, rows, width), bf16),
                dma((count + heads,)),
                dma((count + heads, CHIPS)),
                dma((count + heads,)),
                dma((CHIPS,)),
                dma((count, 3, lay.columns)),
                dma((count, lay.columns)),
                dma((count,)),
                dma((count,)),
                dma((count,)),
                dma((count, CHIPS)),
                pltpu.SemaphoreType.REGULAR,
            ],
            compiler_params=pltpu.CompilerParams(
                collective_id=0, has_side_effects=True, vmem_limit_bytes=59 * 2**20
            ),
            name="group_attention",
        )(live_blocks.T, queries, keys, values)
        return pl.pallas_call(
            hand_out,
            out_shape=jax.ShapeDtypeStruct((rows, hidden), bf16),
            in_specs=[pl.BlockSpec(memory_space=pl.ANY)],
            out_specs=pl.BlockSpec(memory_space=pl.ANY),
            scratch_shapes=[dma((2,))],
            compiler_params=pltpu.CompilerParams(vmem_limit_bytes=2**20),
            name="hand_out",
        )(held)

    spec = P(("blk", "uly"), None)
    return jax.shard_map(
        body, mesh=mesh, in_specs=(spec, spec, spec, P()), out_specs=spec, check_vma=False
    )
```

```python
import math

import jax
import jax.numpy as jnp
from jax import lax
from jax.experimental import pallas as pl
from jax.experimental.pallas import tpu as pltpu
from jax.sharding import PartitionSpec as P

HD = 128
CORES = 2
SIDE = 2
CHIPS = SIDE * SIDE
GROUP = CHIPS * CORES
MESH = pl.DeviceIdType.MESH


class Layout:
    def __init__(self, n_uly, n_blk):
        self.n_uly = n_uly
        self.nx = n_blk // CORES
        self.ny = 2 ** (int(math.log2(n_uly)) // 2)
        self.nz = n_uly // self.ny
        self.columns = n_uly * n_blk // GROUP

    def split(self, uly, blk):
        x, core = blk // CORES, blk % CORES
        z, y = uly // self.ny, uly % self.ny
        column = ((x // SIDE) * (self.ny // SIDE) + y // SIDE) * self.nz + z
        return column, (x % SIDE) * SIDE + y % SIDE, core

    def join(self, column, chip, core):
        z, square = column % self.nz, column // self.nz
        x = (square // (self.ny // SIDE)) * SIDE + chip // SIDE
        y = (square % (self.ny // SIDE)) * SIDE + chip % SIDE
        return z * self.ny + y, x * CORES + core

    def slot(self, block):
        column, chip, core = self.split(block % self.n_uly, block // self.n_uly)
        return column * GROUP + core * CHIPS + chip


def partner(chip, rel):
    a = (chip // 2 + rel // 2) % 2
    b = (chip % 2 + rel % 2) % 2
    return a * 2 + b


def cut(heads):
    pieces = [(head, 0, 0, HD) for head in range(heads)] + [(head, 1, 0, HD) for head in range(heads - 1)]
    low = 0
    for size in (HD // 2, HD // 2):
        pieces.append((heads - 1, 1, low, size))
        low += size
    return pieces


def turns(piece, heads):
    return piece[0] == heads - 1 and piece[1] == 1


def kernel(lay, live_hbm, q_ref, k_ref, v_ref, o_ref,
           live_ref, live_sem, qbuf, bufs, vin, vturn, pbuf, lbuf, obuf,
           plane_send, plane_recv, own_sem, in_sem, z_send, z_recv, c_send, c_recv, o_send, o_recv, pace):
    heads = k_ref.shape[1] // HD // CHIPS
    width = q_ref.shape[1] // CHIPS // heads
    share = width // HD
    live = live_ref.shape[0]
    last = lay.columns - 1
    pieces = cut(heads)
    count = len(pieces)
    turned = [p for p in range(count) if turns(pieces[p], heads)]
    column, chip, core = lay.split(lax.axis_index("uly"), lax.axis_index("blk"))

    def device(col, which, core_of):
        uly, blk = lay.join(col, which, core_of)
        return {"uly": uly, "blk": blk}

    has_down, has_up = column > 0, column < last
    middle = has_down & has_up
    down, up = jnp.maximum(column - 1, 0), jnp.minimum(column + 1, last)
    skips = ((column == 0) & (last > 1), jnp.minimum(column + 2, last)), ((column == last) & (last > 1), jnp.maximum(column - 2, 0))
    skipped = ((column == 2, jnp.maximum(column - 2, 0)), (column == last - 2, jnp.minimum(column + 2, last)))
    beyond = jnp.where(column == 0, skips[0][1], skips[1][1])
    targets = (
        device(down, chip, core), device(up, chip, core), device(beyond, chip, core), device(column, chip, 1 - core)
    )

    barrier = pltpu.get_barrier_semaphore()
    for rel in range(1, CHIPS):
        pl.semaphore_signal(
            barrier, inc=1, device_id=device(column, partner(chip, rel), core), device_id_type=MESH
        )
    pl.semaphore_signal(barrier, inc=1, device_id=targets[3], device_id_type=MESH)

    @pl.when(has_down)
    def _():
        pl.semaphore_signal(barrier, inc=1, device_id=targets[0], device_id_type=MESH)

    @pl.when(has_up)
    def _():
        pl.semaphore_signal(barrier, inc=1, device_id=targets[1], device_id_type=MESH)

    greeted = CHIPS + has_down.astype(jnp.int32) + has_up.astype(jnp.int32)
    for near, col in (*skips, *skipped):
        greeted = greeted + near.astype(jnp.int32)

        @pl.when(near)
        def _():
            pl.semaphore_signal(barrier, inc=1, device_id=device(col, chip, core), device_id_type=MESH)

    def cols(index, size):
        return pl.ds(pl.multiple_of(index * size, size), size)

    def slot_of(col, item, core_of):
        return col * GROUP + core_of * CHIPS + item

    here = slot_of(column, chip, core)

    def route(item, rel):
        if item >= count:
            head = item - count
            src = q_ref.at[:, cols(partner(chip, rel) * heads + head, width)]
            return src, qbuf.at[head, rel]
        head, kind, low, size = pieces[item]
        if item in turned:
            return vturn.at[rel, pl.ds(low, size)], bufs[item].at[here]
        src = (k_ref, v_ref)[kind].at[:, cols(partner(chip, rel) * heads + head, HD)]
        return src, bufs[item].at[here]

    def own(item):
        src, dst = route(item, 0)
        return pltpu.make_async_copy(src, dst, own_sem.at[item])

    def plane(item, rel):
        src, dst = route(item, rel)
        return pltpu.make_async_remote_copy(
            src, dst, plane_send.at[item], plane_recv.at[item, rel],
            device_id=device(column, partner(chip, rel), core), device_id_type=MESH,
        )

    def take(rel):
        src = v_ref.at[:, cols(partner(chip, rel) * heads + heads - 1, HD)]
        return pltpu.make_async_copy(src, vin.at[rel], in_sem.at[rel])

    straight = [p for p in range(count) if p not in turned]

    fetch = pltpu.make_async_copy(live_hbm, live_ref, live_sem)
    for rel in range(CHIPS):
        take(rel).start()
    for item in (*straight, *range(count, count + heads)):
        own(item).start()
    fetch.start()
    pl.semaphore_wait(barrier, greeted)

    def chunk(p, col, core_of):
        return bufs[p].at[pl.ds(slot_of(col, 0, core_of), CHIPS)]

    def hop(p, way, col):
        ref = chunk(p, col, core)
        return pltpu.make_async_remote_copy(
            ref, ref, z_send.at[p, way, col], z_recv.at[p, col],
            device_id=targets[way], device_id_type=MESH,
        )

    def cross(p, col, core_of):
        ref = chunk(p, col, core_of)
        return pltpu.make_async_remote_copy(
            ref, ref, c_send.at[p], c_recv.at[p],
            device_id=targets[3], device_id_type=MESH,
        )

    def leave(p, way, rel):
        ref = bufs[p].at[slot_of(column, partner(chip, rel), core)]
        src = route(p, 0)[0] if rel == 0 else ref
        return pltpu.make_async_remote_copy(
            src, ref, z_send.at[p, way, column], z_recv.at[p, column],
            device_id=targets[way], device_id_type=MESH,
        )

    def leave_both(p, rel):
        @pl.when(has_down)
        def _():
            leave(p, 0, rel).start()

        @pl.when(has_up)
        def _():
            leave(p, 1, rel).start()

        if lay.columns > 2:
            @pl.when((column == 0) | (column == last))
            def _():
                leave(p, 2, rel).start()

    def first(p):
        for rel in range(1, CHIPS):
            plane(p, rel).wait_recv()
            if p == 0:
                leave_both(p, rel)
        own(p).wait()
        if p > 0:
            @pl.when(has_down)
            def _():
                hop(p, 0, column).start()

            @pl.when(has_up)
            def _():
                hop(p, 1, column).start()

            if lay.columns > 2:
                @pl.when((column == 0) | (column == last))
                def _():
                    hop(p, 2, column).start()
        cross(p, column, core).start()

    def forwards_up(col):
        return has_up & jnp.logical_not((col == 0) & (column == 1))

    def forwards_down(col):
        return has_down & jnp.logical_not((col == last) & (column == last - 1))

    def relay(p, step):
        above, below = column + step, column - step

        @pl.when(below >= 0)
        def _():
            hop(p, 1, below).wait_recv()

            @pl.when(forwards_up(below))
            def _():
                hop(p, 1, below).start()

            cross(p, below, core).start()

        @pl.when(above <= last)
        def _():
            hop(p, 0, above).wait_recv()

            @pl.when(forwards_down(above))
            def _():
                hop(p, 0, above).start()

            cross(p, above, core).start()

    def relays(p):
        @pl.loop(1, lay.columns)
        def _(step):
            relay(p, step)

    def bulk(ref, sem):
        return pltpu.make_async_copy(ref, ref, sem)

    def half(p):
        return bufs[p].at[pl.ds(0, lay.columns * CHIPS)]

    def crossed(p):
        bulk(half(p), c_recv.at[p]).wait()

    factor = math.log2(math.e) / math.sqrt(HD)

    def picked(p, rel):
        uly, blk = lay.join(column, partner(chip, rel), core)
        row = blk * lay.n_uly + uly
        axis = 1 if p in turned else 0
        return jnp.concatenate([bufs[p][lay.slot(live_ref[i, row])] for i in range(live)], axis=axis)

    def weigh(p, rel):
        head = pieces[p][0]
        keys = picked(p, rel)
        rows = qbuf.shape[2]
        for r in range(share):
            scores = lax.dot_general(
                qbuf[head, rel, :, r * HD:(r + 1) * HD], keys, (((1,), (1,)), ((), ())),
                preferred_element_type=jnp.float32,
            )
            row_max = jnp.max(scores, axis=1, keepdims=True)
            weights = jnp.exp2((scores - row_max) * factor)
            total = jnp.sum(weights, axis=1, keepdims=True)
            lbuf[head, rel, r * rows:(r + 1) * rows] = jnp.broadcast_to(1 / total, (rows, HD))
            pbuf[head, rel, r * rows:(r + 1) * rows] = weights.astype(jnp.bfloat16)

    def lanes(p):
        head, kind, low, size = pieces[p]
        return pl.ds(low * share, size * share)

    def back(p, rel):
        head, kind, low, size = pieces[p]
        start = pl.multiple_of((chip * heads + head) * width, width) + low * share
        dst = o_ref.at[:, pl.ds(pl.multiple_of(start, HD), size * share)]
        src = obuf.at[head, rel, :, lanes(p)]
        return pltpu.make_async_remote_copy(
            src, dst, o_send.at[p], o_recv.at[p, rel],
            device_id=device(column, partner(chip, rel), core), device_id_type=MESH,
        )

    def keep(head, p):
        return pltpu.make_async_copy(obuf.at[head, 0], o_ref.at[:, cols(chip * heads + head, width)], o_recv.at[p, 0])

    def attend(p, rel):
        head, kind, low, size = pieces[p]
        dims = (((1,), (1 if p in turned else 0,)), ((), ()))
        product = lax.dot_general(pbuf[head, rel], picked(p, rel), dims, preferred_element_type=jnp.float32)
        result = (product * lbuf[head, rel][:, :size]).astype(jnp.bfloat16)
        rows = result.shape[0] // share
        obuf[head, rel, :, lanes(p)] = jnp.concatenate(
            [result[r * rows:(r + 1) * rows] for r in range(share)], axis=1
        )

        @pl.when(rel > 0)
        def _():
            back(p, rel).start()

        if p not in turned:
            @pl.when(rel == 0)
            def _():
                keep(head, p).start()

    def in_order(packed):
        parts = [pieces[p][2:] for p in turned]
        return jnp.concatenate([
            packed[:, low * share + r * size:low * share + (r + 1) * size]
            for r in range(share) for low, size in parts
        ], axis=1)

    def ready(p):
        crossed(p)
        head, kind = pieces[p][:2]
        if kind == 0:
            own(count + head).wait()
            for rel in range(1, CHIPS):
                plane(count + head, rel).wait_recv()

    def units(p, coming=None):
        @pl.loop(0, CHIPS)
        def _(step):
            if p >= 0 and pieces[p][1] == 0:
                weigh(p, step)
            elif p >= 0:
                attend(p, CHIPS - 1 - step)
            if coming is not None:
                @pl.when((step > 0) & jnp.logical_not(middle))
                def _():
                    relay(coming, step)

        if coming is not None and lay.columns > CHIPS:
            @pl.when(jnp.logical_not(middle))
            def _():
                @pl.loop(CHIPS, lay.columns)
                def _(step):
                    relay(coming, step)

    def gone(p):
        @pl.loop(0, lay.columns)
        def _(col):
            @pl.when((col >= column) & forwards_down(col))
            def _():
                hop(p, 0, col).wait_send()

            @pl.when((col <= column) & forwards_up(col))
            def _():
                hop(p, 1, col).wait_send()

    paced = range(turned[0] - 2, count - 2)

    def keep_pace(p):
        gone(p)
        pl.semaphore_signal(pace, inc=1, device_id=targets[3], device_id_type=MESH)
        pl.semaphore_wait(pace, 1)

    def settle():
        for item in range(count + heads):
            ref = bufs[item].at[pl.ds(0, CHIPS - 1)] if item < count else qbuf.at[0, pl.ds(0, CHIPS - 1)]
            bulk(ref, plane_send.at[item]).wait()
        for p in range(count):
            bulk(half(p), c_send.at[p]).wait()

        @pl.when(middle)
        def _():
            for p in range(count):
                if p not in paced:
                    gone(p)

        @pl.when(jnp.logical_not(middle))
        def _():
            for p in range(count):
                @pl.when(has_down)
                def _():
                    hop(p, 0, column).wait_send()

                @pl.when(has_up)
                def _():
                    hop(p, 1, column).wait_send()

                if lay.columns > 2:
                    hop(p, 2, column).wait_send()

    leave_both(0, 0)

    for p in straight:
        for rel in range(1, CHIPS):
            plane(p, rel).start()
    for rel in range(CHIPS):
        take(rel).wait()
        vturn[rel] = vin[rel].T
    for p in turned:
        own(p).start()
        for rel in range(1, CHIPS):
            plane(p, rel).start()
    for head in range(heads):
        for rel in range(1, CHIPS):
            plane(count + head, rel).start()
    first(0)
    fetch.wait()

    @pl.when(jnp.logical_not(middle))
    def _():
        for p in range(1, count):
            first(p)

    for p in range(count):
        @pl.when(middle)
        def _():
            if p == 0:
                first(1)
            relays(p)
            if 0 < p < count - 1:
                if p - 1 in paced:
                    keep_pace(p - 1)
                first(p + 1)

        if p > 0:
            ready(p - 1)
        units(p - 1, p)

    ready(count - 1)
    units(count - 1)


    settle()
    mine = cols(chip * heads + heads - 1, width)
    o_ref[:, mine] = in_order(obuf[heads - 1, 0])

    for p in range(count):
        head, kind = pieces[p][:2]
        if kind == 1 and p not in turned:
            keep(head, p).wait()
            bulk(obuf.at[head, pl.ds(1, CHIPS - 1)], o_send.at[p]).wait()
            for rel in range(1, CHIPS):
                back(p, rel).wait_recv()
    for rel in range(1, CHIPS):
        for p in turned:
            back(p, rel).wait_recv()
        theirs = cols(partner(chip, rel) * heads + heads - 1, width)
        o_ref[:, theirs] = in_order(o_ref[:, theirs])
    for p in turned:
        bulk(obuf.at[heads - 1, pl.ds(1, CHIPS - 1), :, lanes(p)], o_send.at[p]).wait()


def hand_out(src, dst, sem):
    parts = sem.shape[0]
    rows = src.shape[0] // parts
    copies = [
        pltpu.make_async_copy(src.at[pl.ds(i * rows, rows)], dst.at[pl.ds(i * rows, rows)], sem.at[i])
        for i in range(parts)
    ]
    for copy in copies:
        copy.start()
    for copy in copies:
        copy.wait()


def solution(mesh):
    lay = Layout(mesh.shape["uly"], mesh.shape["blk"])

    def body(queries, keys, values, live_blocks):
        rows, hidden = queries.shape
        heads = keys.shape[1] // HD // CHIPS
        width = hidden // CHIPS // heads
        share = width // HD
        slots = lay.columns * GROUP
        count = len(cut(heads))
        keys_seen = live_blocks.shape[1] * rows
        bf16, f32 = jnp.bfloat16, jnp.float32
        dma = pltpu.SemaphoreType.DMA

        def call(*refs):
            kernel(lay, *refs)

        held = pl.pallas_call(
            call,
            out_shape=pltpu.VMEM((rows, hidden), bf16),
            in_specs=[pl.BlockSpec(memory_space=pltpu.HBM)] * 4,
            out_specs=pl.BlockSpec(memory_space=pltpu.VMEM),
            scratch_shapes=[
                pltpu.SMEM(live_blocks.shape[::-1], live_blocks.dtype),
                dma,
                pltpu.VMEM((heads, CHIPS, rows, width), bf16),
                [
                    pltpu.VMEM((slots, *((p[3], rows) if turns(p, heads) else (rows, HD))), bf16)
                    for p in cut(heads)
                ],
                *[pltpu.VMEM((CHIPS, rows, HD), bf16) for _ in range(2)],
                pltpu.VMEM((heads, CHIPS, rows * share, keys_seen), bf16),
                pltpu.VMEM((heads, CHIPS, rows * share, HD), f32),
                pltpu.VMEM((heads, CHIPS, rows, width), bf16),
                dma((count + heads,)),
                dma((count + heads, CHIPS)),
                dma((count + heads,)),
                dma((CHIPS,)),
                dma((count, 3, lay.columns)),
                dma((count, lay.columns)),
                dma((count,)),
                dma((count,)),
                dma((count,)),
                dma((count, CHIPS)),
                pltpu.SemaphoreType.REGULAR,
            ],
            compiler_params=pltpu.CompilerParams(
                collective_id=0, has_side_effects=True, vmem_limit_bytes=59 * 2**20
            ),
            name="group_attention",
        )(live_blocks.T, queries, keys, values)
        return pl.pallas_call(
            hand_out,
            out_shape=jax.ShapeDtypeStruct((rows, hidden), bf16),
            in_specs=[pl.BlockSpec(memory_space=pl.ANY)],
            out_specs=pl.BlockSpec(memory_space=pl.ANY),
            scratch_shapes=[dma((2,))],
            compiler_params=pltpu.CompilerParams(vmem_limit_bytes=2**20),
            name="hand_out",
        )(held)

    spec = P(("blk", "uly"), None)
    return jax.shard_map(
        body, mesh=mesh, in_specs=(spec, spec, spec, P()), out_specs=spec, check_vma=False
    )
```

```python
import math

import jax
import jax.numpy as jnp
from jax import lax
from jax.experimental import pallas as pl
from jax.experimental.pallas import tpu as pltpu
from jax.sharding import PartitionSpec as P

HD = 128
CORES = 2
SIDE = 2
CHIPS = SIDE * SIDE
GROUP = CHIPS * CORES
MESH = pl.DeviceIdType.MESH


class Layout:
    def __init__(self, n_uly, n_blk):
        self.n_uly = n_uly
        self.nx = n_blk // CORES
        self.ny = 2 ** (int(math.log2(n_uly)) // 2)
        self.nz = n_uly // self.ny
        self.columns = n_uly * n_blk // GROUP

    def split(self, uly, blk):
        x, core = blk // CORES, blk % CORES
        z, y = uly // self.ny, uly % self.ny
        column = ((x // SIDE) * (self.ny // SIDE) + y // SIDE) * self.nz + z
        return column, (x % SIDE) * SIDE + y % SIDE, core

    def join(self, column, chip, core):
        z, square = column % self.nz, column // self.nz
        x = (square // (self.ny // SIDE)) * SIDE + chip // SIDE
        y = (square % (self.ny // SIDE)) * SIDE + chip % SIDE
        return z * self.ny + y, x * CORES + core

    def slot(self, block):
        column, chip, core = self.split(block % self.n_uly, block // self.n_uly)
        return column * GROUP + core * CHIPS + chip


def partner(chip, rel):
    a = (chip // 2 + rel // 2) % 2
    b = (chip % 2 + rel % 2) % 2
    return a * 2 + b


def cut(heads):
    pieces = []
    for head in range(heads - 1):
        pieces += [(head, 0, 0, HD), (head, 1, 0, HD)]
    pieces.append((heads - 1, 0, 0, HD))
    low = 0
    for size in (HD // 2, HD // 2):
        pieces.append((heads - 1, 1, low, size))
        low += size
    return pieces


def turns(piece, heads):
    return piece[0] == heads - 1 and piece[1] == 1


def kernel(lay, live_hbm, q_ref, k_ref, v_ref, o_ref,
           live_ref, live_sem, qbuf, bufs, vin, vturn, pbuf, lbuf, obuf,
           plane_send, plane_recv, own_sem, in_sem, z_send, z_recv, c_send, c_recv, o_send, o_recv, pace):
    heads = k_ref.shape[1] // HD // CHIPS
    width = q_ref.shape[1] // CHIPS // heads
    share = width // HD
    live = live_ref.shape[0]
    last = lay.columns - 1
    pieces = cut(heads)
    count = len(pieces)
    turned = [p for p in range(count) if turns(pieces[p], heads)]
    column, chip, core = lay.split(lax.axis_index("uly"), lax.axis_index("blk"))

    def device(col, which, core_of):
        uly, blk = lay.join(col, which, core_of)
        return {"uly": uly, "blk": blk}

    has_down, has_up = column > 0, column < last
    middle = has_down & has_up
    down, up = jnp.maximum(column - 1, 0), jnp.minimum(column + 1, last)
    skips = ((column == 0) & (last > 1), jnp.minimum(column + 2, last)), ((column == last) & (last > 1), jnp.maximum(column - 2, 0))
    skipped = ((column == 2, jnp.maximum(column - 2, 0)), (column == last - 2, jnp.minimum(column + 2, last)))
    beyond = jnp.where(column == 0, skips[0][1], skips[1][1])
    targets = (
        device(down, chip, core), device(up, chip, core), device(beyond, chip, core), device(column, chip, 1 - core)
    )

    barrier = pltpu.get_barrier_semaphore()
    for rel in range(1, CHIPS):
        pl.semaphore_signal(
            barrier, inc=1, device_id=device(column, partner(chip, rel), core), device_id_type=MESH
        )
    pl.semaphore_signal(barrier, inc=1, device_id=targets[3], device_id_type=MESH)

    @pl.when(has_down)
    def _():
        pl.semaphore_signal(barrier, inc=1, device_id=targets[0], device_id_type=MESH)

    @pl.when(has_up)
    def _():
        pl.semaphore_signal(barrier, inc=1, device_id=targets[1], device_id_type=MESH)

    greeted = CHIPS + has_down.astype(jnp.int32) + has_up.astype(jnp.int32)
    for near, col in (*skips, *skipped):
        greeted = greeted + near.astype(jnp.int32)

        @pl.when(near)
        def _():
            pl.semaphore_signal(barrier, inc=1, device_id=device(col, chip, core), device_id_type=MESH)

    def cols(index, size):
        return pl.ds(pl.multiple_of(index * size, size), size)

    def slot_of(col, item, core_of):
        return col * GROUP + core_of * CHIPS + item

    here = slot_of(column, chip, core)

    def route(item, rel):
        if item >= count:
            head = item - count
            src = q_ref.at[:, cols(partner(chip, rel) * heads + head, width)]
            return src, qbuf.at[head, rel]
        head, kind, low, size = pieces[item]
        if item in turned:
            return vturn.at[rel, pl.ds(low, size)], bufs[item].at[here]
        src = (k_ref, v_ref)[kind].at[:, cols(partner(chip, rel) * heads + head, HD)]
        return src, bufs[item].at[here]

    def own(item):
        src, dst = route(item, 0)
        return pltpu.make_async_copy(src, dst, own_sem.at[item])

    def plane(item, rel):
        src, dst = route(item, rel)
        return pltpu.make_async_remote_copy(
            src, dst, plane_send.at[item], plane_recv.at[item, rel],
            device_id=device(column, partner(chip, rel), core), device_id_type=MESH,
        )

    def take(rel):
        src = v_ref.at[:, cols(partner(chip, rel) * heads + heads - 1, HD)]
        return pltpu.make_async_copy(src, vin.at[rel], in_sem.at[rel])

    straight = [p for p in range(count) if p not in turned]

    fetch = pltpu.make_async_copy(live_hbm, live_ref, live_sem)
    for rel in range(CHIPS):
        take(rel).start()
    for item in (*straight, *range(count, count + heads)):
        own(item).start()
    fetch.start()
    pl.semaphore_wait(barrier, greeted)

    def chunk(p, col, core_of):
        return bufs[p].at[pl.ds(slot_of(col, 0, core_of), CHIPS)]

    def hop(p, way, col):
        ref = chunk(p, col, core)
        return pltpu.make_async_remote_copy(
            ref, ref, z_send.at[p, way, col], z_recv.at[p, col],
            device_id=targets[way], device_id_type=MESH,
        )

    def cross(p, col, core_of):
        ref = chunk(p, col, core_of)
        return pltpu.make_async_remote_copy(
            ref, ref, c_send.at[p], c_recv.at[p],
            device_id=targets[3], device_id_type=MESH,
        )

    def leave(p, way, rel):
        ref = bufs[p].at[slot_of(column, partner(chip, rel), core)]
        src = route(p, 0)[0] if rel == 0 else ref
        return pltpu.make_async_remote_copy(
            src, ref, z_send.at[p, way, column], z_recv.at[p, column],
            device_id=targets[way], device_id_type=MESH,
        )

    def leave_both(p, rel):
        @pl.when(has_down)
        def _():
            leave(p, 0, rel).start()

        @pl.when(has_up)
        def _():
            leave(p, 1, rel).start()

        if lay.columns > 2:
            @pl.when((column == 0) | (column == last))
            def _():
                leave(p, 2, rel).start()

    def first(p):
        for rel in range(1, CHIPS):
            plane(p, rel).wait_recv()
            if p == 0:
                leave_both(p, rel)
        own(p).wait()
        if p > 0:
            @pl.when(has_down)
            def _():
                hop(p, 0, column).start()

            @pl.when(has_up)
            def _():
                hop(p, 1, column).start()

            if lay.columns > 2:
                @pl.when((column == 0) | (column == last))
                def _():
                    hop(p, 2, column).start()
        cross(p, column, core).start()

    def forwards_up(col):
        return has_up & jnp.logical_not((col == 0) & (column == 1))

    def forwards_down(col):
        return has_down & jnp.logical_not((col == last) & (column == last - 1))

    def relay(p, step):
        above, below = column + step, column - step

        @pl.when(below >= 0)
        def _():
            hop(p, 1, below).wait_recv()

            @pl.when(forwards_up(below))
            def _():
                hop(p, 1, below).start()

            cross(p, below, core).start()

        @pl.when(above <= last)
        def _():
            hop(p, 0, above).wait_recv()

            @pl.when(forwards_down(above))
            def _():
                hop(p, 0, above).start()

            cross(p, above, core).start()

    def relays(p):
        @pl.loop(1, lay.columns)
        def _(step):
            relay(p, step)

    def bulk(ref, sem):
        return pltpu.make_async_copy(ref, ref, sem)

    def half(p):
        return bufs[p].at[pl.ds(0, lay.columns * CHIPS)]

    def crossed(p):
        bulk(half(p), c_recv.at[p]).wait()

    factor = math.log2(math.e) / math.sqrt(HD)

    def picked(p, rel):
        uly, blk = lay.join(column, partner(chip, rel), core)
        row = blk * lay.n_uly + uly
        axis = 1 if p in turned else 0
        return jnp.concatenate([bufs[p][lay.slot(live_ref[i, row])] for i in range(live)], axis=axis)

    def weigh(p, rel):
        head = pieces[p][0]
        keys = picked(p, rel)
        rows = qbuf.shape[2]
        for r in range(share):
            scores = lax.dot_general(
                qbuf[head, rel, :, r * HD:(r + 1) * HD], keys, (((1,), (1,)), ((), ())),
                preferred_element_type=jnp.float32,
            )
            row_max = jnp.max(scores, axis=1, keepdims=True)
            weights = jnp.exp2((scores - row_max) * factor)
            total = jnp.sum(weights, axis=1, keepdims=True)
            lbuf[rel, r * rows:(r + 1) * rows] = jnp.broadcast_to(1 / total, (rows, HD))
            pbuf[rel, r * rows:(r + 1) * rows] = weights.astype(jnp.bfloat16)

    def lanes(p):
        head, kind, low, size = pieces[p]
        return pl.ds(low * share, size * share)

    def back(p, rel):
        head, kind, low, size = pieces[p]
        start = pl.multiple_of((chip * heads + head) * width, width) + low * share
        dst = o_ref.at[:, pl.ds(pl.multiple_of(start, HD), size * share)]
        src = obuf.at[head, rel, :, lanes(p)]
        return pltpu.make_async_remote_copy(
            src, dst, o_send.at[p], o_recv.at[p, rel],
            device_id=device(column, partner(chip, rel), core), device_id_type=MESH,
        )

    def keep(head, p):
        return pltpu.make_async_copy(obuf.at[head, 0], o_ref.at[:, cols(chip * heads + head, width)], o_recv.at[p, 0])

    def attend(p, rel):
        head, kind, low, size = pieces[p]
        dims = (((1,), (1 if p in turned else 0,)), ((), ()))
        product = lax.dot_general(pbuf[rel], picked(p, rel), dims, preferred_element_type=jnp.float32)
        result = (product * lbuf[rel][:, :size]).astype(jnp.bfloat16)
        rows = result.shape[0] // share
        obuf[head, rel, :, lanes(p)] = jnp.concatenate(
            [result[r * rows:(r + 1) * rows] for r in range(share)], axis=1
        )

        @pl.when(rel > 0)
        def _():
            back(p, rel).start()

        if p not in turned:
            @pl.when(rel == 0)
            def _():
                keep(head, p).start()

    def in_order(packed):
        parts = [pieces[p][2:] for p in turned]
        return jnp.concatenate([
            packed[:, low * share + r * size:low * share + (r + 1) * size]
            for r in range(share) for low, size in parts
        ], axis=1)

    def ready(p):
        crossed(p)
        head, kind = pieces[p][:2]
        if kind == 0:
            own(count + head).wait()
            for rel in range(1, CHIPS):
                plane(count + head, rel).wait_recv()

    def units(p, coming=None):
        @pl.loop(0, CHIPS)
        def _(step):
            if p >= 0 and pieces[p][1] == 0:
                weigh(p, step)
            elif p >= 0:
                attend(p, CHIPS - 1 - step)
            if coming is not None:
                @pl.when((step > 0) & jnp.logical_not(middle))
                def _():
                    relay(coming, step)

        if coming is not None and lay.columns > CHIPS:
            @pl.when(jnp.logical_not(middle))
            def _():
                @pl.loop(CHIPS, lay.columns)
                def _(step):
                    relay(coming, step)

    def gone(p):
        @pl.loop(0, lay.columns)
        def _(col):
            @pl.when((col >= column) & forwards_down(col))
            def _():
                hop(p, 0, col).wait_send()

            @pl.when((col <= column) & forwards_up(col))
            def _():
                hop(p, 1, col).wait_send()

    paced = range(turned[0] - 2, count - 2)

    def keep_pace(p):
        gone(p)
        pl.semaphore_signal(pace, inc=1, device_id=targets[3], device_id_type=MESH)
        pl.semaphore_wait(pace, 1)

    def settle():
        for item in range(count + heads):
            ref = bufs[item].at[pl.ds(0, CHIPS - 1)] if item < count else qbuf.at[0, pl.ds(0, CHIPS - 1)]
            bulk(ref, plane_send.at[item]).wait()
        for p in range(count):
            bulk(half(p), c_send.at[p]).wait()

        @pl.when(middle)
        def _():
            for p in range(count):
                if p not in paced:
                    gone(p)

        @pl.when(jnp.logical_not(middle))
        def _():
            for p in range(count):
                @pl.when(has_down)
                def _():
                    hop(p, 0, column).wait_send()

                @pl.when(has_up)
                def _():
                    hop(p, 1, column).wait_send()

                if lay.columns > 2:
                    hop(p, 2, column).wait_send()

    leave_both(0, 0)

    for p in straight:
        for rel in range(1, CHIPS):
            plane(p, rel).start()
    for rel in range(CHIPS):
        take(rel).wait()
        vturn[rel] = vin[rel].T
    for p in turned:
        own(p).start()
        for rel in range(1, CHIPS):
            plane(p, rel).start()
    for head in range(heads):
        for rel in range(1, CHIPS):
            plane(count + head, rel).start()
    first(0)
    fetch.wait()

    @pl.when(jnp.logical_not(middle))
    def _():
        for p in range(1, count):
            first(p)

    for p in range(count):
        @pl.when(middle)
        def _():
            if p == 0:
                first(1)
            relays(p)
            if 0 < p < count - 1:
                if p - 1 in paced:
                    keep_pace(p - 1)
                first(p + 1)

        if p > 0:
            ready(p - 1)
        units(p - 1, p)

    ready(count - 1)
    units(count - 1)


    settle()
    mine = cols(chip * heads + heads - 1, width)
    o_ref[:, mine] = in_order(obuf[heads - 1, 0])

    for p in range(count):
        head, kind = pieces[p][:2]
        if kind == 1 and p not in turned:
            keep(head, p).wait()
            bulk(obuf.at[head, pl.ds(1, CHIPS - 1)], o_send.at[p]).wait()
            for rel in range(1, CHIPS):
                back(p, rel).wait_recv()
    for rel in range(1, CHIPS):
        for p in turned:
            back(p, rel).wait_recv()
        theirs = cols(partner(chip, rel) * heads + heads - 1, width)
        o_ref[:, theirs] = in_order(o_ref[:, theirs])
    for p in turned:
        bulk(obuf.at[heads - 1, pl.ds(1, CHIPS - 1), :, lanes(p)], o_send.at[p]).wait()


def hand_out(src, dst, sem):
    parts = sem.shape[0]
    rows = src.shape[0] // parts
    copies = [
        pltpu.make_async_copy(src.at[pl.ds(i * rows, rows)], dst.at[pl.ds(i * rows, rows)], sem.at[i])
        for i in range(parts)
    ]
    for copy in copies:
        copy.start()
    for copy in copies:
        copy.wait()


def solution(mesh):
    lay = Layout(mesh.shape["uly"], mesh.shape["blk"])

    def body(queries, keys, values, live_blocks):
        rows, hidden = queries.shape
        heads = keys.shape[1] // HD // CHIPS
        width = hidden // CHIPS // heads
        share = width // HD
        slots = lay.columns * GROUP
        count = len(cut(heads))
        keys_seen = live_blocks.shape[1] * rows
        bf16, f32 = jnp.bfloat16, jnp.float32
        dma = pltpu.SemaphoreType.DMA

        def call(*refs):
            kernel(lay, *refs)

        held = pl.pallas_call(
            call,
            out_shape=pltpu.VMEM((rows, hidden), bf16),
            in_specs=[pl.BlockSpec(memory_space=pltpu.HBM)] * 4,
            out_specs=pl.BlockSpec(memory_space=pltpu.VMEM),
            scratch_shapes=[
                pltpu.SMEM(live_blocks.shape[::-1], live_blocks.dtype),
                dma,
                pltpu.VMEM((heads, CHIPS, rows, width), bf16),
                [
                    pltpu.VMEM((slots, *((p[3], rows) if turns(p, heads) else (rows, HD))), bf16)
                    for p in cut(heads)
                ],
                *[pltpu.VMEM((CHIPS, rows, HD), bf16) for _ in range(2)],
                pltpu.VMEM((CHIPS, rows * share, keys_seen), bf16),
                pltpu.VMEM((CHIPS, rows * share, HD), f32),
                pltpu.VMEM((heads, CHIPS, rows, width), bf16),
                dma((count + heads,)),
                dma((count + heads, CHIPS)),
                dma((count + heads,)),
                dma((CHIPS,)),
                dma((count, 3, lay.columns)),
                dma((count, lay.columns)),
                dma((count,)),
                dma((count,)),
                dma((count,)),
                dma((count, CHIPS)),
                pltpu.SemaphoreType.REGULAR,
            ],
            compiler_params=pltpu.CompilerParams(
                collective_id=0, has_side_effects=True, vmem_limit_bytes=59 * 2**20
            ),
            name="group_attention",
        )(live_blocks.T, queries, keys, values)
        return pl.pallas_call(
            hand_out,
            out_shape=jax.ShapeDtypeStruct((rows, hidden), bf16),
            in_specs=[pl.BlockSpec(memory_space=pl.ANY)],
            out_specs=pl.BlockSpec(memory_space=pl.ANY),
            scratch_shapes=[dma((1,))],
            compiler_params=pltpu.CompilerParams(vmem_limit_bytes=2**20),
            name="hand_out",
        )(held)

    spec = P(("blk", "uly"), None)
    return jax.shard_map(
        body, mesh=mesh, in_specs=(spec, spec, spec, P()), out_specs=spec, check_vma=False
    )
```
